32 devices in a mesh: seq: 16 (over z, x, core), head: 2 (over y).
Axes of the slice: x: 2, y: 2, z: 4, core: 2. Of those that a mesh axis runs over, the one named last changes fastest.
Arguments:
- tokens: bfloat16 [8192, 4096], P('seq'), may hold values from -18 to 18
- norm_gain: float32 [4096], replicated, may hold values from 0.5 to 1.5
- w_query: bfloat16 [4096, 2048], P(None, 'head'), may hold values from -0.0625 to 0.0625
- w_key: bfloat16 [4096, 512], P(None, 'head'), may hold values from -1.90625 to 1.90625
- w_value: bfloat16 [4096, 512], P(None, 'head'), may hold values from -0.09375 to 0.09375
- w_out: bfloat16 [2048, 4096], P('head'), may hold values from -0.125 to 0.125
- window: int32 [16], P('head'), may hold values from 256 to 4096, as said below
- sink_count: int32 [16], P('head'), may hold values from 1 to 4, as said below
- sink_bias: float32 [16], P('head'), may hold values from 4 to 8
Outputs:
- mixed: bfloat16 [8192, 4096], P('seq', 'head')
The draws below stay inside these ranges and needn't reach their ends.
Inputs may be any that keep to these rules, and one draw needn't show every extreme that they name: Some head's window is exactly 4096. `sink_count`: some head's count is exactly 4.
All inputs are finite; a program needn't handle non-finite values.
Results may differ from the reference program's by a relative error of at most 0.0071.
Values may be sent and summed in bfloat16 or wider, within the bound.
No kernel may reach another device: no remote copies, remote signals or barrier semaphores. Data moves between devices by JAX's collectives and lax.ppermute only.
A program may use at most 128 MiB of HBM per device.

```python
import jax
import jax.numpy as jnp
from jax import lax

D = 4096
HEADS = 16
KV_HEADS = 4
HEAD_DIM = 128
SINK = 4
WINMAX = 4096
T_DEV = 512
SPAN = 9
TOKENS = 8192
N_SEQ = 16
N_HEAD = 2


def query_matrix(key):
    base = jax.random.normal(jax.random.fold_in(key, 11), (D, HEADS * HEAD_DIM), jnp.float32)
    return jnp.clip(base, -4.0, 4.0) * D ** (-0.5)


def draw_w_query(key, part):
    return query_matrix(key).astype(jnp.bfloat16)


def draw_w_key(key, part):
    noise = jnp.clip(jax.random.normal(jax.random.fold_in(key, 12), (D, KV_HEADS, HEAD_DIM), jnp.float32), -4.0, 4.0) * D ** (-0.5)
    result = noise
    return result.reshape(D, KV_HEADS * HEAD_DIM).astype(jnp.bfloat16)


def draw_tokens(key, part):
    shape = (TOKENS, D)
    base = jnp.clip(jax.random.normal(jax.random.fold_in(key, 24), shape, jnp.float32), -6.0, 6.0)
    return base.astype(jnp.bfloat16)


def draw_window(key, part):
    lengths = jax.random.randint(jax.random.fold_in(key, 31), (HEADS,), T_DEV // 2, WINMAX + 1, jnp.int32)
    chosen = jax.random.randint(jax.random.fold_in(key, 32), (), 0, HEADS, jnp.int32)
    return jnp.where(jnp.arange(HEADS, dtype=jnp.int32) == chosen, WINMAX, lengths).astype(jnp.int32)


def draw_sink_count(key, part):
    counts = jax.random.randint(jax.random.fold_in(key, 41), (HEADS,), 1, SINK + 1, jnp.int32)
    chosen = jax.random.randint(jax.random.fold_in(key, 42), (), 0, HEADS, jnp.int32)
    return jnp.where(jnp.arange(HEADS, dtype=jnp.int32) == chosen, SINK, counts).astype(jnp.int32)


def shard_levels(stream_key, shape, pieces, low, high):
    level, own = 1.0, jax.random.fold_in(stream_key, 6)
    for dim, shards_of in pieces:
        draws = jnp.exp(jax.random.uniform(jax.random.fold_in(own, dim), (shards_of,), jnp.float32, low / len(pieces), high / len(pieces)))
        level = level * jnp.repeat(draws, shape[dim] // shards_of).reshape([-1 if axis == dim else 1 for axis in range(len(shape))])
    return level


def gaussian(key, dims, scale, limit, cuts=(), held_as=jnp.bfloat16):
    values = scale * jax.random.normal(key, dims, jnp.float32)
    if cuts:
        values = values * shard_levels(key, dims, cuts, -0.22, 0.18)
    return jnp.clip(values, -limit, limit).astype(held_as)


def setup_inputs(seed: int = 0) -> dict:
    keys = jax.random.split(jax.random.key(seed), 10)
    tokens = draw_tokens(jax.random.fold_in(keys[9], 71), 0)
    norm_gain = jnp.clip(1.0 + 0.1 * jax.random.normal(keys[1], (D,), jnp.float32), 0.5, 1.5)
    w_query = draw_w_query(jax.random.fold_in(keys[9], 71), 0)
    w_key = draw_w_key(jax.random.fold_in(keys[9], 71), 0)
    w_value = gaussian(keys[4], (D, KV_HEADS * HEAD_DIM), D ** -0.5, 0.09375, ((1, 2),))
    w_out = gaussian(keys[5], (HEADS * HEAD_DIM, D), (HEADS * HEAD_DIM) ** -0.5, 0.125, ((0, 2),))
    window = draw_window(jax.random.fold_in(keys[9], 71), 0)
    sink_count = draw_sink_count(jax.random.fold_in(keys[9], 71), 0)
    sink_bias = jnp.clip(4.0 + 4.0 * jax.random.uniform(keys[8], (HEADS,), jnp.float32) ** shard_levels(keys[8], (HEADS,), ((0, 2),), -0.2, 0.2), 4.0, 8.0)
    return dict(tokens=tokens, norm_gain=norm_gain, w_query=w_query, w_key=w_key, w_value=w_value, w_out=w_out, window=window, sink_count=sink_count, sink_bias=sink_bias)


EPSILON = 1e-05

def normalize(tokens, norm_gain):
    widened = tokens.astype(jnp.float32)
    row_scale = lax.rsqrt(lax.optimization_barrier(jnp.mean(widened * widened, axis=1, keepdims=True)) + EPSILON)
    return (widened, (widened * row_scale * norm_gain).astype(jnp.bfloat16))

def attend(queries, block_keys, block_values, anchor_key_rows, anchor_value_rows, query_start, key_start, window, sink_count, sink_bias):
    tok_rows, heads_here, head_width = queries.shape
    key_rows, groups_here, _ = block_keys.shape
    per_group = heads_here // groups_here
    query_groups = queries.astype(jnp.float32).reshape(tok_rows, groups_here, per_group, head_width)
    softmax_scale = head_width ** (-0.5)
    scores = jnp.einsum('tgre,lge->grtl', query_groups, block_keys.astype(jnp.float32)) * softmax_scale
    anchor_score_rows = jnp.einsum('yxmo,kxo->xmyk', query_groups, anchor_key_rows.astype(jnp.float32)) * softmax_scale
    anchor_score_rows = anchor_score_rows + sink_bias.reshape(groups_here, per_group)[:, :, None, None]
    query_pos = (query_start + jnp.arange(tok_rows, dtype=jnp.int32))[None, None, :, None]
    key_pos = (key_start + jnp.arange(key_rows, dtype=jnp.int32))[None, None, None, :]
    sink_pos = jnp.arange(anchor_key_rows.shape[0], dtype=jnp.int32)[None, None, None, :]
    reach_rows = window.reshape(groups_here, per_group)[:, :, None, None]
    open_sinks = sink_count.reshape(groups_here, per_group)[:, :, None, None]
    visible = (key_pos <= query_pos) & (key_pos > query_pos - reach_rows) & (key_pos >= 0)
    sink_open = (sink_pos < open_sinks) & (sink_pos <= query_pos - reach_rows)
    scores = jnp.where(visible, scores, -1e+30)
    anchor_score_rows = jnp.where(sink_open, anchor_score_rows, -1e+30)
    peak_score = jnp.maximum(lax.optimization_barrier(jnp.max(scores, axis=3, keepdims=True)), lax.optimization_barrier(jnp.max(anchor_score_rows, axis=3, keepdims=True)))
    weights = jnp.exp(scores - peak_score)
    anchor_weight_rows = jnp.exp(anchor_score_rows - peak_score)
    denominator = lax.optimization_barrier(jnp.sum(weights, axis=3, keepdims=True)) + lax.optimization_barrier(jnp.sum(anchor_weight_rows, axis=3, keepdims=True))
    weights = (weights / denominator).astype(jnp.bfloat16)
    anchor_weight_rows = (anchor_weight_rows / denominator).astype(jnp.bfloat16)
    merged_scores = jnp.einsum('grtl,lge->tgre', weights.astype(jnp.float32), block_values.astype(jnp.float32))
    merged_scores = merged_scores + jnp.einsum('pvlu,upc->lpvc', anchor_weight_rows.astype(jnp.float32), anchor_value_rows.astype(jnp.float32))
    return merged_scores.astype(jnp.bfloat16).reshape(tok_rows, heads_here * head_width)

def reference(tokens, norm_gain, w_query, w_key, w_value, w_out, window, sink_count, sink_bias):
    widened, normed = normalize(tokens, norm_gain)
    total_rows = tokens.shape[0]
    queries = jnp.dot(normed, w_query, preferred_element_type=jnp.float32).astype(jnp.bfloat16).reshape(total_rows, HEADS, HEAD_DIM)
    keys_all = jnp.dot(normed, w_key, preferred_element_type=jnp.float32).astype(jnp.bfloat16).reshape(total_rows, KV_HEADS, HEAD_DIM)
    values_all = jnp.dot(normed, w_value, preferred_element_type=jnp.float32).astype(jnp.bfloat16).reshape(total_rows, KV_HEADS, HEAD_DIM)
    margin = (SPAN - 1) * T_DEV
    padding = jnp.zeros((margin, KV_HEADS, HEAD_DIM), keys_all.dtype)
    padded_keys = jnp.concatenate([padding, keys_all], axis=0)
    padded_values = jnp.concatenate([padding, values_all], axis=0)
    anchor_key_rows = keys_all[:SINK]
    anchor_value_rows = values_all[:SINK]

    def one_block(block_index):
        query_start = (block_index * T_DEV).astype(jnp.int32)
        block_queries = lax.dynamic_slice_in_dim(queries, query_start, T_DEV, 0)
        block_keys = lax.dynamic_slice_in_dim(padded_keys, query_start, SPAN * T_DEV, 0)
        block_values = lax.dynamic_slice_in_dim(padded_values, query_start, SPAN * T_DEV, 0)
        return attend(block_queries, block_keys, block_values, anchor_key_rows, anchor_value_rows, query_start, query_start - margin, window, sink_count, sink_bias)
    attended = lax.map(one_block, jnp.arange(N_SEQ, dtype=jnp.int32)).reshape(total_rows, HEADS * HEAD_DIM)
    half_width = HEADS * HEAD_DIM // N_HEAD
    merged_scores = jnp.zeros((total_rows, D), jnp.float32)
    for part_index in range(N_HEAD):
        lower = part_index * half_width
        partial_term = jnp.dot(attended[:, lower:lower + half_width], w_out[lower:lower + half_width], preferred_element_type=jnp.float32).astype(jnp.bfloat16)
        merged_scores = merged_scores + lax.optimization_barrier(partial_term).astype(jnp.float32)
    return (widened + merged_scores).astype(jnp.bfloat16)
```

```python
import functools

import jax
import jax.numpy as jnp
from jax import lax
from jax.experimental import pallas as pl
from jax.experimental.pallas import tpu as pltpu
from jax.sharding import PartitionSpec as P

HEAD_DIM = 128
SINK = 4
SINK_ROWS = 16
SPAN = 9
QUAD = (SPAN - 1) // 2
EPSILON = 1e-05
LOG2E = 1.4426950408889634
LOW = -1e30
VMEM_LIMIT = 60 * 1024 * 1024
ANY = pl.BlockSpec(memory_space=pl.ANY)
SMEM = pl.BlockSpec(memory_space=pltpu.SMEM)
VMEM = pl.BlockSpec(memory_space=pltpu.VMEM)


def norm_kv_kernel(tok_ref, gain_ref, wk_ref, wv_ref, normed_ref, kv_ref):
    widened = tok_ref[...].astype(jnp.float32)
    row_scale = lax.rsqrt(jnp.mean(widened * widened, axis=1, keepdims=True) + EPSILON)
    normed = (widened * row_scale * gain_ref[...]).astype(jnp.bfloat16)
    normed_ref[...] = normed
    keys = jnp.dot(normed, wk_ref[...], preferred_element_type=jnp.float32).astype(jnp.bfloat16)
    values = jnp.dot(normed, wv_ref[...], preferred_element_type=jnp.float32).astype(jnp.bfloat16)
    for g in range(keys.shape[1] // HEAD_DIM):
        lo = 2 * g * HEAD_DIM
        kv_ref[:, lo : lo + HEAD_DIM] = keys[:, g * HEAD_DIM : (g + 1) * HEAD_DIM]
        kv_ref[:, lo + HEAD_DIM : lo + 2 * HEAD_DIM] = values[:, g * HEAD_DIM : (g + 1) * HEAD_DIM]


def norm_kv(tokens, gain, w_key, w_value):
    rows, width = tokens.shape
    kv_width = w_key.shape[1] + w_value.shape[1]
    tile = rows // 2
    return pl.pallas_call(
        norm_kv_kernel,
        grid=(rows // tile,),
        in_specs=[
            pl.BlockSpec((tile, width), lambda i: (i, 0)),
            pl.BlockSpec((1, width), lambda i: (0, 0)),
            pl.BlockSpec(w_key.shape, lambda i: (0, 0)),
            pl.BlockSpec(w_value.shape, lambda i: (0, 0)),
        ],
        out_specs=[
            pl.BlockSpec((tile, width), lambda i: (i, 0)),
            pl.BlockSpec((tile, kv_width), lambda i: (i, 0)),
        ],
        out_shape=[
            jax.ShapeDtypeStruct((rows, width), jnp.bfloat16),
            jax.ShapeDtypeStruct((rows, kv_width), jnp.bfloat16),
        ],
        compiler_params=pltpu.CompilerParams(vmem_limit_bytes=VMEM_LIMIT),
        cost_estimate=pl.CostEstimate(
            flops=2 * rows * width * kv_width, bytes_accessed=4 * rows * width + 2 * width * kv_width, transcendentals=rows
        ),
        name="norm_kv",
    )(tokens, gain.reshape(1, width), w_key, w_value)


def attend_kernel(group, slots, meta, window, sinks, bias, q_ref, *refs):
    kv_refs, sink_ref, out_ref = refs[:slots], refs[slots], refs[slots + 1]
    kvbuf, m_ref, acc_ref, sems = refs[slots + 2 :]
    rows = q_ref.shape[0]
    key_rows = kvbuf.shape[1]
    heads = q_ref.shape[1] // HEAD_DIM
    cols = pl.ds(2 * group * HEAD_DIM, 2 * HEAD_DIM)
    copies = [
        pltpu.make_async_copy(ref.at[:, cols], kvbuf.at[s, :, pl.ds(0, 2 * HEAD_DIM)], sems.at[s])
        for s, ref in enumerate(kv_refs)
    ]
    for copy in copies:
        copy.start()
    kvbuf[:, :, 2 * HEAD_DIM :] = jnp.ones((slots, key_rows, HEAD_DIM), jnp.bfloat16)
    for copy in copies:
        copy.wait()
    own = meta[0]
    query_start = own * rows
    tile = 256
    diff = lax.broadcasted_iota(jnp.int32, (tile, key_rows), 0) - lax.broadcasted_iota(jnp.int32, (tile, key_rows), 1)

    def update(t, scores, vaug):
        at = pl.ds(t * tile, tile)
        m_prev = m_ref[at, :]
        m_new = jnp.maximum(m_prev, jnp.max(scores, axis=1, keepdims=True))
        alpha = jnp.exp2(m_prev - m_new)
        reps = scores.shape[1] // HEAD_DIM
        weights = jnp.exp2(scores - jnp.concatenate([m_new] * reps, axis=1)).astype(jnp.bfloat16)
        m_ref[at, :] = m_new
        add = jnp.dot(weights, vaug, preferred_element_type=jnp.float32)
        acc_ref[at, :] = acc_ref[at, :] * jnp.concatenate([alpha, alpha], axis=1) + add

    def one_head(index, carry):
        head = pl.ds(pl.multiple_of(index * HEAD_DIM, HEAD_DIM), HEAD_DIM)
        reach = window[group * heads + index]
        m_ref[...] = jnp.full(m_ref.shape, LOW, jnp.float32)
        acc_ref[...] = jnp.zeros(acc_ref.shape, jnp.float32)

        def scores_of(t, keys):
            return lax.dot_general(
                q_ref[pl.ds(t * tile, tile), head], keys, (((1,), (1,)), ((), ())), preferred_element_type=jnp.float32
            )

        def one_slot(s, carry):
            block = meta[1 + s]
            ahead = (own - block) * rows
            some = (block >= 0) & (ahead - (rows - 1) < reach)
            whole = (ahead > 0) & (ahead + rows - 1 < reach)

            @pl.when(some & whole)
            def _():
                keys, vaug = kvbuf[s, :, :HEAD_DIM], kvbuf[s, :, HEAD_DIM:]
                for t in range(rows // tile):
                    update(t, scores_of(t, keys), vaug)

            @pl.when(some & jnp.logical_not(whole))
            def _():
                keys, vaug = kvbuf[s, :, :HEAD_DIM], kvbuf[s, :, HEAD_DIM:]
                for t in range(rows // tile):
                    gap = diff + (ahead + t * tile)
                    scores = jnp.where((gap >= 0) & (gap < reach), scores_of(t, keys), LOW)
                    update(t, scores, vaug)

            return carry

        lax.fori_loop(0, slots, one_slot, 0)

        @pl.when(query_start + rows - 1 - reach >= 0)
        def _():
            base = 2 * group * HEAD_DIM
            pad = jnp.zeros((HEAD_DIM - SINK_ROWS, HEAD_DIM), jnp.bfloat16)
            keys = jnp.concatenate([sink_ref[:, base : base + HEAD_DIM], pad], axis=0)
            values = jnp.concatenate([sink_ref[:, base + HEAD_DIM : base + 2 * HEAD_DIM], pad], axis=0)
            vaug = jnp.concatenate([values, jnp.ones((HEAD_DIM, HEAD_DIM), jnp.bfloat16)], axis=1)
            column = lax.broadcasted_iota(jnp.int32, (tile, HEAD_DIM), 1)
            row = lax.broadcasted_iota(jnp.int32, (tile, HEAD_DIM), 0)
            shift = bias[group * heads + index] * LOG2E
            count = jnp.minimum(sinks[group * heads + index], SINK)
            for t in range(rows // tile):
                latest = row + (query_start + t * tile - reach)
                open_ = (column < count) & (column <= latest)
                update(t, jnp.where(open_, scores_of(t, keys) + shift, LOW), vaug)

        out_ref[:, head] = (acc_ref[:, :HEAD_DIM] / acc_ref[:, HEAD_DIM:]).astype(jnp.bfloat16)
        return carry

    lax.fori_loop(0, heads, one_head, 0)


def attend(group, groups, meta, window, sink_count, sink_bias, queries, blocks, sink_rows):
    rows, width = queries.shape
    share = width // groups
    slots = len(blocks)
    key_rows = blocks[0].shape[0]
    return pl.pallas_call(
        functools.partial(attend_kernel, group, slots),
        grid=(1,),
        in_specs=[SMEM] * 4
        + [pl.BlockSpec((rows, share), lambda i: (0, group))]
        + [ANY] * slots
        + [pl.BlockSpec(sink_rows.shape, lambda i: (0, 0))],
        out_specs=pl.BlockSpec((rows, share), lambda i: (0, 0)),
        out_shape=jax.ShapeDtypeStruct((rows, share), jnp.bfloat16),
        scratch_shapes=[
            pltpu.VMEM((slots, key_rows, 3 * HEAD_DIM), jnp.bfloat16),
            pltpu.VMEM((rows, HEAD_DIM), jnp.float32),
            pltpu.VMEM((rows, 2 * HEAD_DIM), jnp.float32),
            pltpu.SemaphoreType.DMA((slots,)),
        ],
        compiler_params=pltpu.CompilerParams(vmem_limit_bytes=32 * 1024 * 1024),
        cost_estimate=pl.CostEstimate(
            flops=4 * rows * slots * key_rows * share,
            bytes_accessed=2 * slots * key_rows * 2 * HEAD_DIM,
            transcendentals=rows * slots * key_rows * (share // HEAD_DIM),
        ),
        name="attend",
    )(meta, window, sink_count, sink_bias, queries, *blocks, sink_rows)


def project_kernel(where, tok_ref, own0, own1, far0, far1, w_ref, wa_ref, wb_ref, out_ref):
    step = pl.program_id(0)
    half = own0.shape[1]
    total = tok_ref[...].astype(jnp.float32)
    total += jnp.dot(own0[...], w_ref[:half, :], preferred_element_type=jnp.float32)
    total += jnp.dot(own1[...], w_ref[half:, :], preferred_element_type=jnp.float32)

    def finish(w):
        more = jnp.dot(far0[...], w[:half, :], preferred_element_type=jnp.float32)
        more += jnp.dot(far1[...], w[half:, :], preferred_element_type=jnp.float32)
        out_ref[...] = (total + more).astype(jnp.bfloat16)

    @pl.when(step < pl.num_programs(0) // 2)
    def _():
        finish(wa_ref)

    @pl.when(step >= pl.num_programs(0) // 2)
    def _():
        finish(wb_ref)


def project(where, tokens, own, far, w_out, w_near, w_swap):
    rows = tokens.shape[0]
    depth, piece = w_near.shape
    share = 2 * piece
    tile = 512
    steps = share // tile
    part = steps // 2

    def column(j, where):
        return jnp.where(where[1] == 0, j, lax.rem(j + part, steps))

    full = lambda a: pl.BlockSpec(a.shape, lambda j, where: (0, 0))
    shifted_column = lambda j, where: (0, where[0] * steps + column(j, where))
    return pl.pallas_call(
        project_kernel,
        grid_spec=pltpu.PrefetchScalarGridSpec(
            num_scalar_prefetch=1,
            grid=(steps,),
            in_specs=[
                pl.BlockSpec((rows, tile), shifted_column),
                full(own[0]),
                full(own[1]),
                full(far[0]),
                full(far[1]),
                pl.BlockSpec((depth, tile), shifted_column),
                pl.BlockSpec((depth, tile), lambda j, where: (0, jnp.minimum(j, part - 1))),
                pl.BlockSpec((depth, tile), lambda j, where: (0, jnp.maximum(j - part, 0))),
            ],
            out_specs=pl.BlockSpec((rows, tile), lambda j, where: (0, column(j, where))),
        ),
        out_shape=jax.ShapeDtypeStruct((rows, share), jnp.bfloat16),
        compiler_params=pltpu.CompilerParams(vmem_limit_bytes=VMEM_LIMIT),
        cost_estimate=pl.CostEstimate(
            flops=4 * rows * depth * share, bytes_accessed=4 * depth * share + 4 * rows * share, transcendentals=0
        ),
        name="project",
    )(where, tokens, own[0], own[1], far[0], far[1], w_out, w_near, w_swap)


def local(tokens, norm_gain, w_query, w_key, w_value, w_out, window, sink_count, sink_bias):
    peers = lax.axis_size("seq")
    head_peers = lax.axis_size("head")
    me = lax.axis_index("seq")
    my_head = lax.axis_index("head")
    core, side = me % 2, (me // 2) % 2
    groups = w_key.shape[1] // HEAD_DIM
    share = w_out.shape[1] // head_peers
    piece = share // 2

    ahead = [(i, i + QUAD) for i in range(peers - QUAD)]
    core_swap = [(i, i ^ 1) for i in range(peers)]
    side_swap = [(i, i ^ 2) for i in range(peers)]
    head_swap = [(i, i ^ 1) for i in range(head_peers)]

    w_send = lax.dynamic_slice_in_dim(w_out, (1 - my_head) * share + core * piece, piece, 1)
    normed, kv = norm_kv(tokens, norm_gain, w_key, w_value)

    back4 = lax.ppermute(kv, "seq", ahead)
    w_near = lax.ppermute(w_send, "head", head_swap)

    sink_rows = kv[:SINK_ROWS]
    have = peers
    while have > 1:
        step = have // 2
        arrived = lax.ppermute(sink_rows, "seq", [(i, i + step) for i in range(0, peers, have)])
        sink_rows = jnp.where(me % have == step, arrived, sink_rows)
        have = step

    queries = (
        jnp.dot(normed, w_query, preferred_element_type=jnp.float32) * (HEAD_DIM**-0.5 * LOG2E)
    ).astype(jnp.bfloat16)

    back8 = lax.ppermute(back4, "seq", ahead)
    side_a = lax.ppermute(back4, "seq", side_swap)
    side_b = lax.ppermute(jnp.where(side == 0, kv, back8), "seq", side_swap)
    core_a = lax.ppermute(back4, "seq", core_swap)
    core_b = lax.ppermute(jnp.where(core == 0, kv, back8), "seq", core_swap)
    cross_a = lax.ppermute(side_a, "seq", core_swap)
    cross_b = lax.ppermute(side_b, "seq", core_swap)
    w_swap = lax.ppermute(w_near, "seq", core_swap)

    mate = me ^ 1
    across = jnp.where(side == 0, 2, -2)
    twin = jnp.where(core == 0, 1, -1)
    far_b = jnp.where(side == 0, 8, 0)
    blocks = [kv, back4, core_a, core_b, side_a, cross_a, side_b, cross_b, back8]
    index = [
        me,
        me - 4,
        me + twin - 4,
        me + twin - jnp.where(core == 0, 8, 0),
        me + across - 4,
        mate + across - 4,
        me + across - far_b,
        mate + across - far_b,
        me - 8,
    ]
    meta = jnp.stack([me] + index).astype(jnp.int32)
    own, far = [], []
    for g in range(groups):
        att = attend(g, groups, meta, window, sink_count, sink_bias, queries, blocks, sink_rows)
        own.append(att)
        far.append(lax.ppermute(att, "head", head_swap))
    where = jnp.stack([my_head, core]).astype(jnp.int32)
    return project(where, tokens, own, far, w_out, w_near, w_swap)


def solution(mesh):
    in_specs = (
        P("seq", None),
        P(),
        P(None, "head"),
        P(None, "head"),
        P(None, "head"),
        P("head", None),
        P("head"),
        P("head"),
        P("head"),
    )
    out_specs = P("seq", "head")
    return jax.shard_map(local, mesh=mesh, in_specs=in_specs, out_specs=out_specs, check_vma=False)
```

```python
import functools

import jax
import jax.numpy as jnp
from jax import lax
from jax.experimental import pallas as pl
from jax.experimental.pallas import tpu as pltpu
from jax.sharding import PartitionSpec as P


HEAD_DIM = 128
PAIR = 2 * HEAD_DIM
SINK = 4
SINK_ROWS = 16
SPAN = 9
QUAD = (SPAN - 1) // 2
EPSILON = 1e-05
LOG2E = 1.4426950408889634
LOW = -1e30
UNROLL = 2
MIB = 1024 * 1024
ANY = pl.BlockSpec(memory_space=pl.ANY)
SMEM = pl.BlockSpec(memory_space=pltpu.SMEM)


def keys_values_kernel(place, tok_ref, gain_ref, wk_ref, wv_ref, w_hbm, *refs):
    groups = wk_ref.shape[1] // HEAD_DIM
    kv_refs, (sink_ref, scale_ref, send_hbm) = refs[:groups], refs[groups : groups + 3]
    k_acc, v_acc, squares, w_vmem, sem_in, sem_out = refs[groups + 3 :]
    step, steps = pl.program_id(0), pl.num_programs(0)
    piece = send_hbm.shape[1]
    columns = pl.ds(pl.multiple_of(place[0], HEAD_DIM), piece)
    fetch = pltpu.make_async_copy(w_hbm.at[:, columns], w_vmem, sem_in)
    store = pltpu.make_async_copy(w_vmem, send_hbm, sem_out)

    @pl.when(step == 0)
    def _():
        fetch.start()
        k_acc[...] = jnp.zeros(k_acc.shape, jnp.float32)
        v_acc[...] = jnp.zeros(v_acc.shape, jnp.float32)
        squares[...] = jnp.zeros(squares.shape, jnp.float32)

    @pl.when(step == steps // 2)
    def _():
        fetch.wait()
        store.start()

    widened = tok_ref[...].astype(jnp.float32)
    scaled = (widened * gain_ref[...]).astype(jnp.bfloat16)
    k_acc[...] += jnp.dot(scaled, wk_ref[...], preferred_element_type=jnp.float32)
    v_acc[...] += jnp.dot(scaled, wv_ref[...], preferred_element_type=jnp.float32)
    square = widened * widened
    total = square[:, :HEAD_DIM]
    for lo in range(HEAD_DIM, square.shape[1], HEAD_DIM):
        total += square[:, lo : lo + HEAD_DIM]
    squares[...] += total

    @pl.when(step == steps - 1)
    def _():
        mean = jnp.sum(squares[...], axis=1, keepdims=True) / (steps * tok_ref.shape[1])
        scale = jnp.broadcast_to(lax.rsqrt(mean + EPSILON), scale_ref.shape)
        scale_ref[...] = scale
        for g in range(groups):
            at = slice(g * HEAD_DIM, (g + 1) * HEAD_DIM)
            pair = jnp.concatenate([k_acc[:, at] * scale, v_acc[:, at] * scale], axis=1).astype(jnp.bfloat16)
            kv_refs[g][...] = pair
            sink_ref[:, g * PAIR : (g + 1) * PAIR] = pair[:SINK_ROWS]
        store.wait()


def keys_values(place, tokens, gain, w_key, w_value, w_out, piece):
    rows, width = tokens.shape
    narrow = w_key.shape[1]
    groups = narrow // HEAD_DIM
    chunk = width // 4
    fixed = lambda shape: pl.BlockSpec(shape, lambda i, place: (0, 0))
    return pl.pallas_call(
        keys_values_kernel,
        grid_spec=pltpu.PrefetchScalarGridSpec(
            num_scalar_prefetch=1,
            grid=(width // chunk,),
            in_specs=[
                pl.BlockSpec((rows, chunk), lambda i, place: (0, i)),
                pl.BlockSpec((1, chunk), lambda i, place: (0, i)),
                pl.BlockSpec((chunk, narrow), lambda i, place: (i, 0)),
                pl.BlockSpec((chunk, narrow), lambda i, place: (i, 0)),
                ANY,
            ],
            out_specs=[fixed((rows, PAIR))] * groups
            + [fixed((SINK_ROWS, groups * PAIR)), fixed((rows, HEAD_DIM)), ANY],
            scratch_shapes=[
                pltpu.VMEM((rows, narrow), jnp.float32),
                pltpu.VMEM((rows, narrow), jnp.float32),
                pltpu.VMEM((rows, HEAD_DIM), jnp.float32),
                pltpu.VMEM((w_out.shape[0], piece), jnp.bfloat16),
                pltpu.SemaphoreType.DMA,
                pltpu.SemaphoreType.DMA,
            ],
        ),
        out_shape=[jax.ShapeDtypeStruct((rows, PAIR), jnp.bfloat16)] * groups
        + [
            jax.ShapeDtypeStruct((SINK_ROWS, groups * PAIR), jnp.bfloat16),
            jax.ShapeDtypeStruct((rows, HEAD_DIM), jnp.float32),
            jax.ShapeDtypeStruct((w_out.shape[0], piece), jnp.bfloat16),
        ],
        compiler_params=pltpu.CompilerParams(vmem_limit_bytes=60 * MIB),
        cost_estimate=pl.CostEstimate(
            flops=4 * rows * width * narrow, bytes_accessed=2 * width * (rows + 2 * narrow), transcendentals=rows
        ),
        name="keys_values",
    )(place, tokens, gain, w_key, w_value, w_out)


def query_kernel(tok_ref, gain_ref, w_ref, scale_ref, q_ref, acc):
    step = pl.program_id(0)
    scaled = (tok_ref[...].astype(jnp.float32) * gain_ref[...]).astype(jnp.bfloat16)
    add = jnp.dot(scaled, w_ref[...], preferred_element_type=jnp.float32)

    @pl.when(step == 0)
    def _():
        acc[...] = add

    @pl.when(step > 0)
    def _():
        acc[...] += add

    @pl.when(step == pl.num_programs(0) - 1)
    def _():
        scale = scale_ref[...] * (HEAD_DIM**-0.5 * LOG2E)
        scale = jnp.concatenate([scale] * (acc.shape[1] // HEAD_DIM), axis=1)
        q_ref[...] = (acc[...] * scale).astype(jnp.bfloat16)


def query_group(group, groups, tokens, gain, w_query, scale):
    rows, width = tokens.shape
    share = w_query.shape[1] // groups
    chunk = width // 4
    return pl.pallas_call(
        query_kernel,
        grid=(width // chunk,),
        in_specs=[
            pl.BlockSpec((rows, chunk), lambda i: (0, i)),
            pl.BlockSpec((1, chunk), lambda i: (0, i)),
            pl.BlockSpec((chunk, share), lambda i: (i, group)),
            pl.BlockSpec(scale.shape, lambda i: (0, 0)),
        ],
        out_specs=pl.BlockSpec((rows, share), lambda i: (0, 0)),
        out_shape=jax.ShapeDtypeStruct((rows, share), jnp.bfloat16),
        scratch_shapes=[pltpu.VMEM((rows, share), jnp.float32)],
        compiler_params=pltpu.CompilerParams(vmem_limit_bytes=58 * MIB),
        cost_estimate=pl.CostEstimate(
            flops=2 * rows * width * share, bytes_accessed=2 * width * (rows + share), transcendentals=0
        ),
        name="query_group",
    )(tokens, gain, w_query, scale)


def attend_kernel(group, slots, meta, window, sinks, bias, q_ref, *refs):
    kv_refs, sink_ref, out_ref = refs[:slots], refs[slots], refs[slots + 1]
    kvbuf, sems, masked_items, whole_items, s_even, s_odd, x_even, x_odd, m_ref, acc_ref = refs[slots + 2 :]
    bufs = ((s_even, x_even), (s_odd, x_odd))
    rows = q_ref.shape[0]
    key_rows = kvbuf.shape[1]
    heads = q_ref.shape[1] // HEAD_DIM
    lanes = key_rows // HEAD_DIM
    copies = [
        pltpu.make_async_copy(ref, kvbuf.at[s, :, pl.ds(0, PAIR)], sems.at[s]) for s, ref in enumerate(kv_refs)
    ]
    for copy in copies:
        copy.start()
    kvbuf[:, :, PAIR:] = jnp.ones((slots, key_rows, HEAD_DIM), jnp.bfloat16)
    m_ref[...] = jnp.full(m_ref.shape, LOW, jnp.float32)
    acc_ref[...] = jnp.zeros(acc_ref.shape, jnp.float32)
    own = meta[0]
    query_start = own * rows

    def put(items, n, head, slot, gap):
        items[0, n] = head
        items[1, n] = slot
        items[2, n] = gap

    def scan(s, counts):
        block = meta[1 + s]
        gap = (own - block) * rows

        def add(head, counts):
            masked, whole = counts
            reach = window[group * heads + head]
            put(masked_items, masked, head, s, gap)
            put(whole_items, whole, head, s, gap)
            some = gap - (rows - 1) < reach
            full = (gap > 0) & (gap + rows - 1 < reach)
            return (
                masked + (some & jnp.logical_not(full)).astype(jnp.int32),
                whole + full.astype(jnp.int32),
            )

        return lax.fori_loop(0, jnp.where(block >= 0, heads, 0), add, counts)

    masked, whole = lax.fori_loop(0, slots, scan, (jnp.int32(0), jnp.int32(0)))
    for extra in range(UNROLL):
        put(masked_items, masked + extra, 0, 0, -rows)
        put(whole_items, whole + extra, 0, 0, -rows)
    diff = lax.broadcasted_iota(jnp.int32, (rows, key_rows), 0) - lax.broadcasted_iota(
        jnp.int32, (rows, key_rows), 1
    )
    for copy in copies:
        copy.wait()

    def queries_of(head):
        return q_ref[:, pl.ds(pl.multiple_of(head * HEAD_DIM, HEAD_DIM), HEAD_DIM)]

    def scores_of(head, keys):
        return lax.dot_general(
            queries_of(head), keys, (((1,), (1,)), ((), ())), preferred_element_type=jnp.float32
        )

    def score(items, i, buf, mask):
        head, slot = items[0, i], items[1, i]
        scores = scores_of(head, kvbuf[slot, :, :HEAD_DIM])
        if mask:
            gap = diff + items[2, i]
            scores = jnp.where((gap >= 0) & (gap < window[group * heads + head]), scores, LOW)
        buf[0][...] = scores
        top = scores[:, :HEAD_DIM]
        for part in range(1, lanes):
            top = jnp.maximum(top, scores[:, part * HEAD_DIM : (part + 1) * HEAD_DIM])
        buf[1][...] = top

    def fold(head, scores, top, vaug):
        m_prev = m_ref[head]
        m_new = jnp.maximum(m_prev, jnp.max(top, axis=1, keepdims=True))
        alpha = jnp.exp2(m_prev - m_new)
        m_ref[head] = m_new
        shift = jnp.concatenate([m_new] * (scores.shape[1] // HEAD_DIM), axis=1)
        weights = jnp.exp2(scores - shift).astype(jnp.bfloat16)
        add = jnp.dot(weights, vaug, preferred_element_type=jnp.float32)
        acc_ref[head] = acc_ref[head] * jnp.concatenate([alpha, alpha], axis=1) + add

    def consume(items, i, buf):
        fold(items[0, i], buf[0][...], buf[1][...], kvbuf[items[1, i], :, HEAD_DIM:])

    def turns(items, first, count, mask):
        score(items, first, bufs[0], mask)

        def turn(j, carry):
            for u in range(UNROLL):
                i = first + UNROLL * j + u
                score(items, i + 1, bufs[(u + 1) % 2], mask)
                consume(items, i, bufs[u % 2])
            return carry

        lax.fori_loop(0, count, turn, 0)

    turns(masked_items, 0, (masked + UNROLL - 1) // UNROLL, True)
    rest = lax.rem(whole, UNROLL)

    def single(i, carry):
        score(whole_items, i, bufs[0], False)
        consume(whole_items, i, bufs[0])
        return carry

    lax.fori_loop(0, rest, single, 0)
    turns(whole_items, rest, whole // UNROLL, False)

    def finish(head, carry):
        reach = window[group * heads + head]

        @pl.when(query_start + rows - 1 - reach >= 0)
        def _():
            base = group * PAIR
            pad = jnp.zeros((HEAD_DIM - SINK_ROWS, HEAD_DIM), jnp.bfloat16)
            keys = jnp.concatenate([sink_ref[:, base : base + HEAD_DIM], pad], axis=0)
            values = jnp.concatenate([sink_ref[:, base + HEAD_DIM : base + PAIR], pad], axis=0)
            vaug = jnp.concatenate([values, jnp.ones((HEAD_DIM, HEAD_DIM), jnp.bfloat16)], axis=1)
            column = lax.broadcasted_iota(jnp.int32, (rows, HEAD_DIM), 1)
            latest = lax.broadcasted_iota(jnp.int32, (rows, HEAD_DIM), 0) + (query_start - reach)
            count = jnp.minimum(sinks[group * heads + head], SINK)
            allowed = (column < count) & (column <= latest)
            scores = scores_of(head, keys) + bias[group * heads + head] * LOG2E
            scores = jnp.where(allowed, scores, LOW)
            fold(head, scores, scores, vaug)

        out_ref[:, pl.ds(pl.multiple_of(head * HEAD_DIM, HEAD_DIM), HEAD_DIM)] = (
            acc_ref[head, :, :HEAD_DIM] / acc_ref[head, :, HEAD_DIM:]
        ).astype(jnp.bfloat16)
        return carry

    lax.fori_loop(0, heads, finish, 0)


def attend(group, meta, window, sink_count, sink_bias, queries, blocks, sink_rows):
    rows, share = queries.shape
    heads = share // HEAD_DIM
    slots = len(blocks)
    key_rows = blocks[0].shape[0]
    items = heads * slots + 2 * UNROLL
    f32 = jnp.float32
    return pl.pallas_call(
        functools.partial(attend_kernel, group, slots),
        grid=(1,),
        in_specs=[SMEM] * 4
        + [pl.BlockSpec((rows, share), lambda i: (0, 0))]
        + [ANY] * slots
        + [pl.BlockSpec(sink_rows.shape, lambda i: (0, 0))],
        out_specs=pl.BlockSpec((rows, share), lambda i: (0, 0)),
        out_shape=jax.ShapeDtypeStruct((rows, share), jnp.bfloat16),
        scratch_shapes=[
            pltpu.VMEM((slots, key_rows, 3 * HEAD_DIM), jnp.bfloat16),
            pltpu.SemaphoreType.DMA((slots,)),
            pltpu.SMEM((3, items), jnp.int32),
            pltpu.SMEM((3, items), jnp.int32),
            pltpu.VMEM((rows, key_rows), f32),
            pltpu.VMEM((rows, key_rows), f32),
            pltpu.VMEM((rows, HEAD_DIM), f32),
            pltpu.VMEM((rows, HEAD_DIM), f32),
            pltpu.VMEM((heads, rows, HEAD_DIM), f32),
            pltpu.VMEM((heads, rows, PAIR), f32),
        ],
        compiler_params=pltpu.CompilerParams(vmem_limit_bytes=60 * MIB),
        cost_estimate=pl.CostEstimate(
            flops=8 * rows * SPAN * key_rows * share,
            bytes_accessed=2 * slots * key_rows * PAIR,
            transcendentals=rows * SPAN * key_rows * heads,
        ),
        name="attend",
    )(meta, window, sink_count, sink_bias, queries, *blocks, sink_rows)


def project_kernel(where, tok_ref, own0, own1, w_ref, out_ref):
    half = own0.shape[1]
    total = jnp.dot(own0[...], w_ref[:half, :], preferred_element_type=jnp.float32)
    total += jnp.dot(own1[...], w_ref[half:, :], preferred_element_type=jnp.float32)
    out_ref[...] = tok_ref[...].astype(jnp.float32) + total


def project_last_kernel(where, part_ref, far0, far1, wa_ref, wb_ref, out_ref):
    step = pl.program_id(0)
    half = far0.shape[1]

    def finish(w):
        more = jnp.dot(far0[...], w[:half, :], preferred_element_type=jnp.float32)
        more += jnp.dot(far1[...], w[half:, :], preferred_element_type=jnp.float32)
        out_ref[...] = (part_ref[...] + more).astype(jnp.bfloat16)

    @pl.when(step < pl.num_programs(0) // 2)
    def _():
        finish(wa_ref)

    @pl.when(step >= pl.num_programs(0) // 2)
    def _():
        finish(wb_ref)


def project(where, tokens, own, w_out, share):
    rows = tokens.shape[0]
    depth = w_out.shape[0]
    tile = 512
    steps = share // tile
    shifted = lambda j, where: (0, where[0] * steps + j)
    fixed = lambda a: pl.BlockSpec(a.shape, lambda j, where: (0, 0))
    return pl.pallas_call(
        project_kernel,
        grid_spec=pltpu.PrefetchScalarGridSpec(
            num_scalar_prefetch=1,
            grid=(steps,),
            in_specs=[pl.BlockSpec((rows, tile), shifted), fixed(own[0]), fixed(own[1])]
            + [pl.BlockSpec((depth, tile), shifted)],
            out_specs=pl.BlockSpec((rows, tile), lambda j, where: (0, j)),
        ),
        out_shape=jax.ShapeDtypeStruct((rows, share), jnp.float32),
        compiler_params=pltpu.CompilerParams(vmem_limit_bytes=40 * MIB),
        cost_estimate=pl.CostEstimate(
            flops=2 * rows * depth * share, bytes_accessed=2 * depth * share + 6 * rows * share, transcendentals=0
        ),
        name="project",
    )(where, tokens, own[0], own[1], w_out)


def project_last(where, partial, far, w_near, w_swap):
    rows, share = partial.shape
    depth, _ = w_near.shape
    tile = 512
    steps = share // tile
    part = steps // 2

    def here(j, where):
        return (0, jnp.where(where[1] == 0, j, lax.rem(j + part, steps)))

    fixed = lambda a: pl.BlockSpec(a.shape, lambda j, where: (0, 0))
    return pl.pallas_call(
        project_last_kernel,
        grid_spec=pltpu.PrefetchScalarGridSpec(
            num_scalar_prefetch=1,
            grid=(steps,),
            in_specs=[
                pl.BlockSpec((rows, tile), here),
                fixed(far[0]),
                fixed(far[1]),
                pl.BlockSpec((depth, tile), lambda j, where: (0, jnp.minimum(j, part - 1))),
                pl.BlockSpec((depth, tile), lambda j, where: (0, jnp.maximum(j - part, 0))),
            ],
            out_specs=pl.BlockSpec((rows, tile), here),
        ),
        out_shape=jax.ShapeDtypeStruct((rows, share), jnp.bfloat16),
        compiler_params=pltpu.CompilerParams(vmem_limit_bytes=40 * MIB),
        cost_estimate=pl.CostEstimate(
            flops=2 * rows * depth * share, bytes_accessed=2 * depth * share + 6 * rows * share, transcendentals=0
        ),
        name="project_last",
    )(where, partial, far[0], far[1], w_near, w_swap)


def local(tokens, norm_gain, w_query, w_key, w_value, w_out, window, sink_count, sink_bias):
    peers = lax.axis_size("seq")
    head_peers = lax.axis_size("head")
    me = lax.axis_index("seq")
    my_head = lax.axis_index("head")
    core, side = me % 2, (me // 2) % 2
    groups = w_key.shape[1] // HEAD_DIM
    share = w_out.shape[1] // head_peers
    piece = share // 2
    gain = norm_gain.reshape(1, -1)
    everyone = range(peers)

    def send(x, pairs, axis="seq"):
        return lax.ppermute(x, axis, pairs)

    ahead = [(i, i + QUAD) for i in range(peers - QUAD)]
    core_swap = [(i, i ^ 1) for i in everyone]
    core_up = [(i, i + 1) for i in everyone if i % 2 == 0]
    core_down = [(i, i - 1) for i in everyone if i % 2 == 1]
    side_swap = [(i, i ^ 2) for i in everyone]
    side_up = [(i, i + 2) for i in everyone if (i // 2) % 2 == 0]
    side_down = [(i, i - 2) for i in everyone if (i // 2) % 2 == 1]
    cross_up = [(i, i ^ 1) for i in everyone if (i // 2) % 2 == 1]
    cross_down = [(i, i ^ 1) for i in everyone if (i // 2) % 2 == 0]
    head_swap = [(i, i ^ 1) for i in range(head_peers)]

    twin, across, mirror = me ^ 1, me ^ 2, me ^ 3
    index = [
        me,
        me - 4,
        twin - 4,
        jnp.where(core == 1, me - 1, -1),
        jnp.where(core == 0, me - 7, -1),
        across - 4,
        mirror - 4,
        jnp.where(side == 1, me - 2, -1),
        jnp.where(side == 0, me - 6, -1),
        jnp.where(side == 1, twin - 2, -1),
        jnp.where(side == 0, twin - 6, -1),
        me - 8,
    ]
    meta = jnp.stack([me] + index).astype(jnp.int32)
    place = ((1 - my_head) * share + core * piece).astype(jnp.int32).reshape(1)

    *kv, sink_rows, scale, w_send = keys_values(place, tokens, gain, w_key, w_value, w_out, piece)

    back4 = [send(x, ahead) for x in kv]
    near_side = [send(x, side_up) for x in kv]
    near_core = [send(x, core_up) for x in kv]
    w_near = send(w_send, head_swap, "head")

    def spread(rows, have):
        step = have // 2
        arrived = send(rows, [(i, i + step) for i in range(0, peers, have)])
        return jnp.where(me % have == step, arrived, rows), step

    have = peers
    queries, blocks = [], []
    for g in range(groups):
        queries.append(query_group(g, groups, tokens, gain, w_query, scale))
        b4, ns = back4[g], near_side[g]
        b8 = send(b4, ahead)
        across4 = send(b4, side_swap)
        far_side = send(b8, side_down)
        blocks.append(
            [
                kv[g],
                b4,
                send(b4, core_swap),
                near_core[g],
                send(b8, core_down),
                across4,
                send(across4, core_swap),
                ns,
                far_side,
                send(ns, cross_up),
                send(far_side, cross_down),
                b8,
            ]
        )
    while have > 1:
        sink_rows, have = spread(sink_rows, have)
    w_swap = send(w_near, core_swap)

    own, far = [], []
    for g in range(groups):
        att = attend(g, meta, window, sink_count, sink_bias, queries[g], blocks[g], sink_rows)
        own.append(att)
        far.append(send(att, head_swap, "head"))
    where = jnp.stack([my_head, core]).astype(jnp.int32)
    partial = project(where, tokens, own, w_out, share)
    return project_last(where, partial, far, w_near, w_swap)


def solution(mesh):
    in_specs = (
        P("seq", None),
        P(),
        P(None, "head"),
        P(None, "head"),
        P(None, "head"),
        P("head", None),
        P("head"),
        P("head"),
        P("head"),
    )
    out_specs = P("seq", "head")
    return jax.shard_map(local, mesh=mesh, in_specs=in_specs, out_specs=out_specs, check_vma=False)
```

```python
import functools

import jax
import jax.numpy as jnp
from jax import lax
from jax.experimental import pallas as pl
from jax.experimental.pallas import tpu as pltpu
from jax.sharding import PartitionSpec as P


HEAD_DIM = 128
PAIR = 2 * HEAD_DIM
SINK = 4
SINK_ROWS = 16
SPAN = 9
QUAD = (SPAN - 1) // 2
EPSILON = 1e-05
LOG2E = 1.4426950408889634
LOW = -1e30
UNROLL = 2
MIB = 1024 * 1024
ANY = pl.BlockSpec(memory_space=pl.ANY)
SMEM = pl.BlockSpec(memory_space=pltpu.SMEM)


def keys_values_kernel(place, tok_ref, gain_ref, wk_ref, wv_ref, w_hbm, *refs):
    groups = wk_ref.shape[1] // HEAD_DIM
    kv_refs, (sink_ref, scale_ref, send_hbm) = refs[:groups], refs[groups : groups + 3]
    k_acc, v_acc, squares, w_vmem, sem_in, sem_out = refs[groups + 3 :]
    step, steps = pl.program_id(0), pl.num_programs(0)
    piece = send_hbm.shape[1]
    columns = pl.ds(pl.multiple_of(place[0], HEAD_DIM), piece)
    fetch = pltpu.make_async_copy(w_hbm.at[:, columns], w_vmem, sem_in)
    store = pltpu.make_async_copy(w_vmem, send_hbm, sem_out)

    @pl.when(step == 0)
    def _():
        fetch.start()
        k_acc[...] = jnp.zeros(k_acc.shape, jnp.float32)
        v_acc[...] = jnp.zeros(v_acc.shape, jnp.float32)
        squares[...] = jnp.zeros(squares.shape, jnp.float32)

    @pl.when(step == steps // 2)
    def _():
        fetch.wait()
        store.start()

    widened = tok_ref[...].astype(jnp.float32)
    scaled = (widened * gain_ref[...]).astype(jnp.bfloat16)
    k_acc[...] += jnp.dot(scaled, wk_ref[...], preferred_element_type=jnp.float32)
    v_acc[...] += jnp.dot(scaled, wv_ref[...], preferred_element_type=jnp.float32)
    square = widened * widened
    total = square[:, :HEAD_DIM]
    for lo in range(HEAD_DIM, square.shape[1], HEAD_DIM):
        total += square[:, lo : lo + HEAD_DIM]
    squares[...] += total

    @pl.when(step == steps - 1)
    def _():
        mean = jnp.sum(squares[...], axis=1, keepdims=True) / (steps * tok_ref.shape[1])
        scale = jnp.broadcast_to(lax.rsqrt(mean + EPSILON), scale_ref.shape)
        scale_ref[...] = scale
        for g in range(groups):
            at = slice(g * HEAD_DIM, (g + 1) * HEAD_DIM)
            pair = jnp.concatenate([k_acc[:, at] * scale, v_acc[:, at] * scale], axis=1).astype(jnp.bfloat16)
            kv_refs[g][...] = pair
            sink_ref[:, g * PAIR : (g + 1) * PAIR] = pair[:SINK_ROWS]
        store.wait()


def keys_values(place, tokens, gain, w_key, w_value, w_out, piece):
    rows, width = tokens.shape
    narrow = w_key.shape[1]
    groups = narrow // HEAD_DIM
    chunk = width // 4
    fixed = lambda shape: pl.BlockSpec(shape, lambda i, place: (0, 0))
    return pl.pallas_call(
        keys_values_kernel,
        grid_spec=pltpu.PrefetchScalarGridSpec(
            num_scalar_prefetch=1,
            grid=(width // chunk,),
            in_specs=[
                pl.BlockSpec((rows, chunk), lambda i, place: (0, i)),
                pl.BlockSpec((1, chunk), lambda i, place: (0, i)),
                pl.BlockSpec((chunk, narrow), lambda i, place: (i, 0)),
                pl.BlockSpec((chunk, narrow), lambda i, place: (i, 0)),
                ANY,
            ],
            out_specs=[fixed((rows, PAIR))] * groups
            + [fixed((SINK_ROWS, groups * PAIR)), fixed((rows, HEAD_DIM)), ANY],
            scratch_shapes=[
                pltpu.VMEM((rows, narrow), jnp.float32),
                pltpu.VMEM((rows, narrow), jnp.float32),
                pltpu.VMEM((rows, HEAD_DIM), jnp.float32),
                pltpu.VMEM((w_out.shape[0], piece), jnp.bfloat16),
                pltpu.SemaphoreType.DMA,
                pltpu.SemaphoreType.DMA,
            ],
        ),
        out_shape=[jax.ShapeDtypeStruct((rows, PAIR), jnp.bfloat16)] * groups
        + [
            jax.ShapeDtypeStruct((SINK_ROWS, groups * PAIR), jnp.bfloat16),
            jax.ShapeDtypeStruct((rows, HEAD_DIM), jnp.float32),
            jax.ShapeDtypeStruct((w_out.shape[0], piece), jnp.bfloat16),
        ],
        compiler_params=pltpu.CompilerParams(vmem_limit_bytes=60 * MIB),
        cost_estimate=pl.CostEstimate(
            flops=4 * rows * width * narrow, bytes_accessed=2 * width * (rows + 2 * narrow), transcendentals=rows
        ),
        name="keys_values",
    )(place, tokens, gain, w_key, w_value, w_out)


def query_kernel(tok_ref, gain_ref, w_ref, scale_ref, q_ref, acc):
    step = pl.program_id(0)
    scaled = (tok_ref[...].astype(jnp.float32) * gain_ref[...]).astype(jnp.bfloat16)
    add = jnp.dot(scaled, w_ref[...], preferred_element_type=jnp.float32)

    @pl.when(step == 0)
    def _():
        acc[...] = add

    @pl.when(step > 0)
    def _():
        acc[...] += add

    @pl.when(step == pl.num_programs(0) - 1)
    def _():
        scale = scale_ref[...] * (HEAD_DIM**-0.5 * LOG2E)
        scale = jnp.concatenate([scale] * (acc.shape[1] // HEAD_DIM), axis=1)
        q_ref[...] = (acc[...] * scale).astype(jnp.bfloat16)


def query_group(group, groups, tokens, gain, w_query, scale):
    rows, width = tokens.shape
    share = w_query.shape[1] // groups
    chunk = width // 4
    return pl.pallas_call(
        query_kernel,
        grid=(width // chunk,),
        in_specs=[
            pl.BlockSpec((rows, chunk), lambda i: (0, i)),
            pl.BlockSpec((1, chunk), lambda i: (0, i)),
            pl.BlockSpec((chunk, share), lambda i: (i, group)),
            pl.BlockSpec(scale.shape, lambda i: (0, 0)),
        ],
        out_specs=pl.BlockSpec((rows, share), lambda i: (0, 0)),
        out_shape=jax.ShapeDtypeStruct((rows, share), jnp.bfloat16),
        scratch_shapes=[pltpu.VMEM((rows, share), jnp.float32)],
        compiler_params=pltpu.CompilerParams(vmem_limit_bytes=58 * MIB),
        cost_estimate=pl.CostEstimate(
            flops=2 * rows * width * share, bytes_accessed=2 * width * (rows + share), transcendentals=0
        ),
        name="query_group",
    )(tokens, gain, w_query, scale)


def attend_kernel(group, slots, meta, window, sinks, bias, q_ref, *refs):
    kv_refs, sink_ref, out_ref = refs[:slots], refs[slots], refs[slots + 1]
    kvbuf, sems, masked_items, whole_items, s_even, s_odd, x_even, x_odd, m_ref, acc_ref = refs[slots + 2 :]
    bufs = ((s_even, x_even), (s_odd, x_odd))
    rows = q_ref.shape[0]
    key_rows = kvbuf.shape[1]
    heads = q_ref.shape[1] // HEAD_DIM
    lanes = key_rows // HEAD_DIM
    copies = [
        pltpu.make_async_copy(ref, kvbuf.at[s, :, pl.ds(0, PAIR)], sems.at[s]) for s, ref in enumerate(kv_refs)
    ]
    for copy in copies:
        copy.start()
    kvbuf[:, :, PAIR:] = jnp.ones((slots, key_rows, HEAD_DIM), jnp.bfloat16)
    m_ref[...] = jnp.full(m_ref.shape, LOW, jnp.float32)
    acc_ref[...] = jnp.zeros(acc_ref.shape, jnp.float32)
    own = meta[0]
    query_start = own * rows

    def put(items, n, head, slot, gap):
        items[0, n] = head
        items[1, n] = slot
        items[2, n] = gap

    def scan(s, counts):
        block = meta[1 + s]
        gap = (own - block) * rows

        def add(head, counts):
            masked, whole = counts
            reach = window[group * heads + head]
            put(masked_items, masked, head, s, gap)
            put(whole_items, whole, head, s, gap)
            some = gap - (rows - 1) < reach
            full = (gap > 0) & (gap + rows - 1 < reach)
            return (
                masked + (some & jnp.logical_not(full)).astype(jnp.int32),
                whole + full.astype(jnp.int32),
            )

        return lax.fori_loop(0, jnp.where(block >= 0, heads, 0), add, counts)

    masked, whole = lax.fori_loop(0, slots, scan, (jnp.int32(0), jnp.int32(0)))
    for extra in range(UNROLL):
        put(masked_items, masked + extra, 0, 0, -rows)
        put(whole_items, whole + extra, 0, 0, -rows)
    diff = lax.broadcasted_iota(jnp.int32, (rows, key_rows), 0) - lax.broadcasted_iota(
        jnp.int32, (rows, key_rows), 1
    )
    for copy in copies:
        copy.wait()

    def queries_of(head):
        if isinstance(head, int):
            return q_ref[:, head * HEAD_DIM : (head + 1) * HEAD_DIM]
        return q_ref[:, pl.ds(pl.multiple_of(head * HEAD_DIM, HEAD_DIM), HEAD_DIM)]

    def scores_of(head, keys):
        return lax.dot_general(
            queries_of(head), keys, (((1,), (1,)), ((), ())), preferred_element_type=jnp.float32
        )

    def score(items, i, buf, mask):
        head, slot = items[0, i], items[1, i]
        scores = scores_of(head, kvbuf[slot, :, :HEAD_DIM])
        if mask:
            gap = diff + items[2, i]
            scores = jnp.where((gap >= 0) & (gap < window[group * heads + head]), scores, LOW)
        buf[0][...] = scores
        top = scores[:, :HEAD_DIM]
        for part in range(1, lanes):
            top = jnp.maximum(top, scores[:, part * HEAD_DIM : (part + 1) * HEAD_DIM])
        buf[1][...] = top

    def fold(head, scores, top, vaug):
        m_prev = m_ref[head]
        m_new = jnp.maximum(m_prev, jnp.max(top, axis=1, keepdims=True))
        alpha = jnp.exp2(m_prev - m_new)
        m_ref[head] = m_new
        shift = jnp.concatenate([m_new] * (scores.shape[1] // HEAD_DIM), axis=1)
        weights = jnp.exp2(scores - shift).astype(jnp.bfloat16)
        add = jnp.dot(weights, vaug, preferred_element_type=jnp.float32)
        acc_ref[head] = acc_ref[head] * jnp.concatenate([alpha, alpha], axis=1) + add

    def consume(items, i, buf):
        fold(items[0, i], buf[0][...], buf[1][...], kvbuf[items[1, i], :, HEAD_DIM:])

    def turns(items, first, count, mask):
        score(items, first, bufs[0], mask)

        def turn(j, carry):
            for u in range(UNROLL):
                i = first + UNROLL * j + u
                score(items, i + 1, bufs[(u + 1) % 2], mask)
                consume(items, i, bufs[u % 2])
            return carry

        lax.fori_loop(0, count, turn, 0)

    turns(masked_items, 0, (masked + UNROLL - 1) // UNROLL, True)
    rest = lax.rem(whole, UNROLL)

    def single(i, carry):
        score(whole_items, i, bufs[0], False)
        consume(whole_items, i, bufs[0])
        return carry

    lax.fori_loop(0, rest, single, 0)
    turns(whole_items, rest, whole // UNROLL, False)

    def finish(head):
        out_ref[:, head * HEAD_DIM : (head + 1) * HEAD_DIM] = (
            acc_ref[head, :, :HEAD_DIM] / acc_ref[head, :, HEAD_DIM:]
        ).astype(jnp.bfloat16)

    shortest = window[group * heads]
    for head in range(1, heads):
        shortest = jnp.minimum(shortest, window[group * heads + head])
    any_open = query_start + rows - 1 - shortest >= 0

    @pl.when(any_open)
    def _():
        base = group * PAIR
        pad = jnp.zeros((HEAD_DIM - SINK_ROWS, HEAD_DIM), jnp.bfloat16)
        keys = jnp.concatenate([sink_ref[:, base : base + HEAD_DIM], pad], axis=0)
        values = jnp.concatenate([sink_ref[:, base + HEAD_DIM : base + PAIR], pad], axis=0)
        vaug = jnp.concatenate([values, jnp.ones((HEAD_DIM, HEAD_DIM), jnp.bfloat16)], axis=1)
        column = lax.broadcasted_iota(jnp.int32, (rows, HEAD_DIM), 1)
        row = lax.broadcasted_iota(jnp.int32, (rows, HEAD_DIM), 0)
        scored = []
        for head in range(heads):
            latest = row + (query_start - window[group * heads + head])
            count = jnp.minimum(sinks[group * heads + head], SINK)
            allowed = (column < count) & (column <= latest)
            scores = scores_of(head, keys) + bias[group * heads + head] * LOG2E
            scored.append(jnp.where(allowed, scores, LOW))
        for head in range(heads):
            fold(head, scored[head], scored[head], vaug)
        for head in range(heads):
            finish(head)

    @pl.when(jnp.logical_not(any_open))
    def _():
        for head in range(heads):
            finish(head)


def attend(group, meta, window, sink_count, sink_bias, queries, blocks, sink_rows):
    rows, share = queries.shape
    heads = share // HEAD_DIM
    slots = len(blocks)
    key_rows = blocks[0].shape[0]
    items = heads * slots + 2 * UNROLL
    f32 = jnp.float32
    return pl.pallas_call(
        functools.partial(attend_kernel, group, slots),
        grid=(1,),
        in_specs=[SMEM] * 4
        + [pl.BlockSpec((rows, share), lambda i: (0, 0))]
        + [ANY] * slots
        + [pl.BlockSpec(sink_rows.shape, lambda i: (0, 0))],
        out_specs=pl.BlockSpec((rows, share), lambda i: (0, 0)),
        out_shape=jax.ShapeDtypeStruct((rows, share), jnp.bfloat16),
        scratch_shapes=[
            pltpu.VMEM((slots, key_rows, 3 * HEAD_DIM), jnp.bfloat16),
            pltpu.SemaphoreType.DMA((slots,)),
            pltpu.SMEM((3, items), jnp.int32),
            pltpu.SMEM((3, items), jnp.int32),
            pltpu.VMEM((rows, key_rows), f32),
            pltpu.VMEM((rows, key_rows), f32),
            pltpu.VMEM((rows, HEAD_DIM), f32),
            pltpu.VMEM((rows, HEAD_DIM), f32),
            pltpu.VMEM((heads, rows, HEAD_DIM), f32),
            pltpu.VMEM((heads, rows, PAIR), f32),
        ],
        compiler_params=pltpu.CompilerParams(vmem_limit_bytes=60 * MIB),
        cost_estimate=pl.CostEstimate(
            flops=8 * rows * SPAN * key_rows * share,
            bytes_accessed=2 * slots * key_rows * PAIR,
            transcendentals=rows * SPAN * key_rows * heads,
        ),
        name="attend",
    )(meta, window, sink_count, sink_bias, queries, *blocks, sink_rows)


def project_kernel(where, tok_ref, own0, own1, w_ref, out_ref):
    half = own0.shape[1]
    total = jnp.dot(own0[...], w_ref[:half, :], preferred_element_type=jnp.float32)
    total += jnp.dot(own1[...], w_ref[half:, :], preferred_element_type=jnp.float32)
    out_ref[...] = tok_ref[...].astype(jnp.float32) + total


def project_last_kernel(where, part_ref, far0, far1, wa_ref, wb_ref, out_ref):
    step = pl.program_id(0)
    half = far0.shape[1]

    def finish(w):
        more = jnp.dot(far0[...], w[:half, :], preferred_element_type=jnp.float32)
        more += jnp.dot(far1[...], w[half:, :], preferred_element_type=jnp.float32)
        out_ref[...] = (part_ref[...] + more).astype(jnp.bfloat16)

    @pl.when(step < pl.num_programs(0) // 2)
    def _():
        finish(wa_ref)

    @pl.when(step >= pl.num_programs(0) // 2)
    def _():
        finish(wb_ref)


def project(where, tokens, own, w_out, share):
    rows = tokens.shape[0]
    depth = w_out.shape[0]
    tile = 512
    steps = share // tile
    shifted = lambda j, where: (0, where[0] * steps + j)
    fixed = lambda a: pl.BlockSpec(a.shape, lambda j, where: (0, 0))
    return pl.pallas_call(
        project_kernel,
        grid_spec=pltpu.PrefetchScalarGridSpec(
            num_scalar_prefetch=1,
            grid=(steps,),
            in_specs=[pl.BlockSpec((rows, tile), shifted), fixed(own[0]), fixed(own[1])]
            + [pl.BlockSpec((depth, tile), shifted)],
            out_specs=pl.BlockSpec((rows, tile), lambda j, where: (0, j)),
        ),
        out_shape=jax.ShapeDtypeStruct((rows, share), jnp.float32),
        compiler_params=pltpu.CompilerParams(vmem_limit_bytes=40 * MIB),
        cost_estimate=pl.CostEstimate(
            flops=2 * rows * depth * share, bytes_accessed=2 * depth * share + 6 * rows * share, transcendentals=0
        ),
        name="project",
    )(where, tokens, own[0], own[1], w_out)


def project_last(where, partial, far, w_near, w_swap):
    rows, share = partial.shape
    depth, _ = w_near.shape
    tile = 512
    steps = share // tile
    part = steps // 2

    def here(j, where):
        return (0, jnp.where(where[1] == 0, j, lax.rem(j + part, steps)))

    fixed = lambda a: pl.BlockSpec(a.shape, lambda j, where: (0, 0))
    return pl.pallas_call(
        project_last_kernel,
        grid_spec=pltpu.PrefetchScalarGridSpec(
            num_scalar_prefetch=1,
            grid=(steps,),
            in_specs=[
                pl.BlockSpec((rows, tile), here),
                fixed(far[0]),
                fixed(far[1]),
                pl.BlockSpec((depth, tile), lambda j, where: (0, jnp.minimum(j, part - 1))),
                pl.BlockSpec((depth, tile), lambda j, where: (0, jnp.maximum(j - part, 0))),
            ],
            out_specs=pl.BlockSpec((rows, tile), here),
        ),
        out_shape=jax.ShapeDtypeStruct((rows, share), jnp.bfloat16),
        compiler_params=pltpu.CompilerParams(vmem_limit_bytes=40 * MIB),
        cost_estimate=pl.CostEstimate(
            flops=2 * rows * depth * share, bytes_accessed=2 * depth * share + 6 * rows * share, transcendentals=0
        ),
        name="project_last",
    )(where, partial, far[0], far[1], w_near, w_swap)


def local(tokens, norm_gain, w_query, w_key, w_value, w_out, window, sink_count, sink_bias):
    peers = lax.axis_size("seq")
    head_peers = lax.axis_size("head")
    me = lax.axis_index("seq")
    my_head = lax.axis_index("head")
    core, side = me % 2, (me // 2) % 2
    groups = w_key.shape[1] // HEAD_DIM
    share = w_out.shape[1] // head_peers
    piece = share // 2
    gain = norm_gain.reshape(1, -1)
    everyone = range(peers)

    def send(x, pairs, axis="seq"):
        return lax.ppermute(x, axis, pairs)

    ahead = [(i, (i + QUAD) % peers) for i in everyone]
    core_swap = [(i, i ^ 1) for i in everyone]
    side_swap = [(i, i ^ 2) for i in everyone]
    head_swap = [(i, i ^ 1) for i in range(head_peers)]

    twin, across, mirror = me ^ 1, me ^ 2, me ^ 3
    index = [
        me,
        me - 4,
        twin - 4,
        jnp.where(core == 1, twin, -1),
        jnp.where(core == 0, twin - 8, -1),
        across - 4,
        mirror - 4,
        jnp.where(side == 1, across, -1),
        jnp.where(side == 0, across - 8, -1),
        jnp.where(side == 1, mirror, -1),
        jnp.where(side == 0, mirror - 8, -1),
        me - 8,
    ]
    meta = jnp.stack([me] + index).astype(jnp.int32)
    place = ((1 - my_head) * share + core * piece).astype(jnp.int32).reshape(1)

    *kv, sink_rows, scale, w_send = keys_values(place, tokens, gain, w_key, w_value, w_out, piece)

    back4 = [send(x, ahead) for x in kv]
    near_side = [send(x, side_swap) for x in kv]
    near_core = [send(x, core_swap) for x in kv]
    w_near = send(w_send, head_swap, "head")

    def spread(rows, have):
        step = have // 2
        arrived = send(rows, [(i, (i + step) % peers) for i in everyone])
        return jnp.where(me % have == step, arrived, rows), step

    have = peers
    queries, blocks = [], []
    for g in range(groups):
        queries.append(query_group(g, groups, tokens, gain, w_query, scale))
        b4, ns = back4[g], near_side[g]
        b8 = send(b4, ahead)
        across4 = send(b4, side_swap)
        far_side = send(b8, side_swap)
        blocks.append(
            [
                kv[g],
                b4,
                send(b4, core_swap),
                near_core[g],
                send(b8, core_swap),
                across4,
                send(across4, core_swap),
                ns,
                far_side,
                send(ns, core_swap),
                send(far_side, core_swap),
                b8,
            ]
        )
    while have > 1:
        sink_rows, have = spread(sink_rows, have)
    w_swap = send(w_near, core_swap)

    own, far = [], []
    for g in range(groups):
        att = attend(g, meta, window, sink_count, sink_bias, queries[g], blocks[g], sink_rows)
        own.append(att)
        far.append(send(att, head_swap, "head"))
    where = jnp.stack([my_head, core]).astype(jnp.int32)
    partial = project(where, tokens, own, w_out, share)
    return project_last(where, partial, far, w_near, w_swap)


def solution(mesh):
    in_specs = (
        P("seq", None),
        P(),
        P(None, "head"),
        P(None, "head"),
        P(None, "head"),
        P("head", None),
        P("head"),
        P("head"),
        P("head"),
    )
    out_specs = P("seq", "head")
    return jax.shard_map(local, mesh=mesh, in_specs=in_specs, out_specs=out_specs, check_vma=False)
```

```python
import functools

import jax
import jax.numpy as jnp
from jax import lax
from jax.experimental import pallas as pl
from jax.experimental.pallas import tpu as pltpu
from jax.sharding import PartitionSpec as P


HEAD_DIM = 128
PAIR = 2 * HEAD_DIM
SINK = 4
SINK_ROWS = 16
SPAN = 9
QUAD = (SPAN - 1) // 2
EPSILON = 1e-05
LOG2E = 1.4426950408889634
LOW = -1e30
UNROLL = 2
NOWHERE = 1 << 20
MIB = 1024 * 1024
ALL_VMEM = 67043328 - 128 * 1024
ANY = pl.BlockSpec(memory_space=pltpu.HBM)
SMEM = pl.BlockSpec(memory_space=pltpu.SMEM)


def keys_values_kernel(place, tok_ref, gain_ref, wk_ref, wv_ref, w_hbm, *refs):
    groups = wk_ref.shape[1] // HEAD_DIM
    kv_ref, scale_ref, send_hbm, k_acc, v_acc, squares, w_vmem, sem_in, sem_out = refs
    step, steps = pl.program_id(0), pl.num_programs(0)
    piece = send_hbm.shape[1]
    columns = pl.ds(pl.multiple_of(place[0], HEAD_DIM), piece)
    fetch = pltpu.make_async_copy(w_hbm.at[:, columns], w_vmem, sem_in)
    store = pltpu.make_async_copy(w_vmem, send_hbm, sem_out)

    @pl.when(step == 0)
    def _():
        fetch.start()
        k_acc[...] = jnp.zeros(k_acc.shape, jnp.float32)
        v_acc[...] = jnp.zeros(v_acc.shape, jnp.float32)
        squares[...] = jnp.zeros(squares.shape, jnp.float32)

    @pl.when(step == steps // 2)
    def _():
        fetch.wait()
        store.start()

    widened = tok_ref[...].astype(jnp.float32)
    scaled = (widened * gain_ref[...]).astype(jnp.bfloat16)
    k_acc[...] += jnp.dot(scaled, wk_ref[...], preferred_element_type=jnp.float32)
    v_acc[...] += jnp.dot(scaled, wv_ref[...], preferred_element_type=jnp.float32)
    square = widened * widened
    total = square[:, :HEAD_DIM]
    for lo in range(HEAD_DIM, square.shape[1], HEAD_DIM):
        total += square[:, lo : lo + HEAD_DIM]
    squares[...] += total

    @pl.when(step == steps - 1)
    def _():
        mean = jnp.sum(squares[...], axis=1, keepdims=True) / (steps * tok_ref.shape[1])
        scale = jnp.broadcast_to(lax.rsqrt(mean + EPSILON), scale_ref.shape)
        scale_ref[...] = scale
        for g in range(groups):
            at = slice(g * HEAD_DIM, (g + 1) * HEAD_DIM)
            pair = jnp.concatenate([k_acc[:, at] * scale, v_acc[:, at] * scale], axis=1).astype(jnp.bfloat16)
            kv_ref[:, g * PAIR : (g + 1) * PAIR] = pair
        store.wait()


def keys_values(place, tokens, gain, w_key, w_value, w_out, piece):
    rows, width = tokens.shape
    narrow = w_key.shape[1]
    groups = narrow // HEAD_DIM
    chunk = width // 4
    fixed = lambda shape: pl.BlockSpec(shape, lambda i, place: (0, 0))
    return pl.pallas_call(
        keys_values_kernel,
        grid_spec=pltpu.PrefetchScalarGridSpec(
            num_scalar_prefetch=1,
            grid=(width // chunk,),
            in_specs=[
                pl.BlockSpec((rows, chunk), lambda i, place: (0, i)),
                pl.BlockSpec((1, chunk), lambda i, place: (0, i)),
                pl.BlockSpec((chunk, narrow), lambda i, place: (i, 0)),
                pl.BlockSpec((chunk, narrow), lambda i, place: (i, 0)),
                ANY,
            ],
            out_specs=[fixed((rows, groups * PAIR))]
            + [fixed((rows, HEAD_DIM)), ANY],
            scratch_shapes=[
                pltpu.VMEM((rows, narrow), jnp.float32),
                pltpu.VMEM((rows, narrow), jnp.float32),
                pltpu.VMEM((rows, HEAD_DIM), jnp.float32),
                pltpu.VMEM((w_out.shape[0], piece), jnp.bfloat16),
                pltpu.SemaphoreType.DMA,
                pltpu.SemaphoreType.DMA,
            ],
        ),
        out_shape=[jax.ShapeDtypeStruct((rows, groups * PAIR), jnp.bfloat16)]
        + [
            jax.ShapeDtypeStruct((rows, HEAD_DIM), jnp.float32),
            jax.ShapeDtypeStruct((w_out.shape[0], piece), jnp.bfloat16),
        ],
        compiler_params=pltpu.CompilerParams(vmem_limit_bytes=60 * MIB),
        cost_estimate=pl.CostEstimate(
            flops=4 * rows * width * narrow, bytes_accessed=2 * width * (rows + 2 * narrow), transcendentals=rows
        ),
        name="keys_values",
    )(place, tokens, gain, w_key, w_value, w_out)


def query_kernel(tok_ref, gain_ref, w_ref, scale_ref, q_ref, acc):
    step = pl.program_id(0)
    scaled = (tok_ref[...].astype(jnp.float32) * gain_ref[...]).astype(jnp.bfloat16)
    add = jnp.dot(scaled, w_ref[...], preferred_element_type=jnp.float32)

    @pl.when(step == 0)
    def _():
        acc[...] = add

    @pl.when(step > 0)
    def _():
        acc[...] += add

    @pl.when(step == pl.num_programs(0) - 1)
    def _():
        scale = scale_ref[...] * (HEAD_DIM**-0.5 * LOG2E)
        scale = jnp.concatenate([scale] * (acc.shape[1] // HEAD_DIM), axis=1)
        q_ref[...] = (acc[...] * scale).astype(jnp.bfloat16)


def project_queries(tokens, gain, w_query, scale):
    rows, width = tokens.shape
    share = w_query.shape[1]
    chunk = width // 4
    return pl.pallas_call(
        query_kernel,
        grid=(width // chunk,),
        in_specs=[
            pl.BlockSpec((rows, chunk), lambda i: (0, i)),
            pl.BlockSpec((1, chunk), lambda i: (0, i)),
            pl.BlockSpec((chunk, share), lambda i: (i, 0)),
            pl.BlockSpec(scale.shape, lambda i: (0, 0)),
        ],
        out_specs=pl.BlockSpec((rows, share), lambda i: (0, 0)),
        out_shape=jax.ShapeDtypeStruct((rows, share), jnp.bfloat16),
        scratch_shapes=[pltpu.VMEM((rows, share), jnp.float32)],
        compiler_params=pltpu.CompilerParams(vmem_limit_bytes=58 * MIB),
        cost_estimate=pl.CostEstimate(
            flops=2 * rows * width * share, bytes_accessed=2 * width * (rows + share), transcendentals=0
        ),
        name="queries",
    )(tokens, gain, w_query, scale)


def early_blocks(me):
    twin, core = me ^ 1, me % 2
    return [me, me - 4, jnp.where(core == 0, twin - 4, -1), jnp.where(core == 1, twin, -1)]


def late_blocks(me):
    twin, across, mirror = me ^ 1, me ^ 2, me ^ 3
    core, side = me % 2, (me // 2) % 2
    return [
        me - 8,
        across - 4,
        mirror - 4,
        jnp.where(core == 0, twin - 8, -1),
        jnp.where(side == 1, across, -1),
        jnp.where(side == 1, mirror, -1),
        jnp.where(core == 1, twin - 4, -1),
        jnp.where(side == 0, across - 8, -1),
        jnp.where(side == 0, mirror - 8, -1),
    ]


def attend_kernel(groups, per_group, sources, start, *refs):
    window, sinks, bias, q_hbm = refs[:4]
    sent = 1 + max(ref for slot in sources for ref, _ in slot)
    kv_refs, refs = refs[4 : 4 + sent], refs[4 + sent :]
    if start:
        acc_hbm, packed_hbm = refs[:2]
        refs = refs[2:]
    else:
        sink_old, sink_new, acc_hbm, packed_hbm, out_hbm, sink_ref, out_ref = refs[:5] + refs[-2:]
        refs = refs[5:-2]
    q_ref, kvbuf, sems, items, s_even, s_odd, x_even, x_odd, m_ref, acc_ref, packed_ref = refs
    bufs = ((s_even, x_even), (s_odd, x_odd))
    rows, key_rows = q_ref.shape[0], kvbuf.shape[1]
    share, buffers = len(groups), kvbuf.shape[0]
    heads = share * per_group
    base_head = groups[0] * per_group
    all_heads = acc_hbm.shape[0]
    lanes = key_rows // HEAD_DIM
    own = lax.axis_index("seq")
    query_start = own * rows
    table = early_blocks(own) if start else late_blocks(own)
    acc_vmem = acc_ref.at[:, :, pl.ds(0, HEAD_DIM)]
    copies = [
        pltpu.make_async_copy(
            q_hbm.at[:, pl.ds(base_head * HEAD_DIM, heads * HEAD_DIM)], q_ref, sems.at[buffers]
        )
    ]
    if not start:
        copies += [
            pltpu.make_async_copy(acc_hbm.at[pl.ds(base_head, heads)], acc_vmem, sems.at[buffers + 1]),
            pltpu.make_async_copy(packed_hbm, packed_ref, sems.at[buffers + 2]),
            pltpu.make_async_copy(sink_old, sink_ref.at[0], sems.at[buffers + 3]),
            pltpu.make_async_copy(sink_new, sink_ref.at[1], sems.at[buffers + 4]),
        ]
    longest = [window[base_head + g * per_group] for g in range(share)]
    for g in range(share):
        for head in range(1, per_group):
            longest[g] = jnp.maximum(longest[g], window[base_head + g * per_group + head])
    wanted = []
    for s, slot in enumerate(sources):
        for g, (ref, column) in enumerate(slot):
            need = (table[s] >= 0) & ((own - table[s]) * rows - (rows - 1) < longest[g])
            copy = pltpu.make_async_copy(
                kv_refs[ref].at[:, pl.ds(column, PAIR)],
                kvbuf.at[s * share + g, :, pl.ds(0, PAIR)],
                sems.at[s * share + g],
            )
            wanted.append((need, copy))
            pl.when(need)(copy.start)
    for copy in copies:
        copy.start()
    kvbuf[:, :, PAIR:] = jnp.ones((buffers, key_rows, HEAD_DIM), jnp.bfloat16)
    if start:
        m_ref[...] = jnp.full(m_ref.shape, LOW, jnp.float32)
        acc_ref[...] = jnp.zeros(acc_ref.shape, jnp.float32)

    def put(n, head, kv, gap):
        items[0, n] = head
        items[1, n] = kv
        items[2, n] = gap

    def scan(s, block, n, want_whole):
        gap = (own - block) * rows

        def add(head, n):
            reach = window[base_head + head]
            put(n, head, s * share + head // per_group, gap)
            some = gap - (rows - 1) < reach
            whole = (gap > 0) & (gap + rows - 1 < reach)
            return n + (whole if want_whole else some & jnp.logical_not(whole)).astype(jnp.int32)

        return lax.fori_loop(0, jnp.where(block >= 0, heads, 0), add, n)

    n = jnp.int32(0)
    for s, block in enumerate(table):
        n = scan(s, block, n, False)
    masked = n
    for s, block in enumerate(table):
        n = scan(s, block, n, True)
    odd = lax.rem(n, UNROLL)

    @pl.when(odd > 0)
    def _():
        loaded = items[1, 0]

        def shift(k, carry):
            for row in range(3):
                items[row, n - k] = items[row, n - k - 1]
            return carry

        lax.fori_loop(0, n - masked, shift, 0)
        put(masked, 0, loaded, NOWHERE)

    masked_turns = (masked + odd + UNROLL - 1) // UNROLL
    all_turns = (n + odd) // UNROLL
    put(n + odd, 0, 0, NOWHERE)
    diff = lax.broadcasted_iota(jnp.int32, (rows, key_rows), 0) - lax.broadcasted_iota(
        jnp.int32, (rows, key_rows), 1
    )
    for copy in copies:
        copy.wait()
    for need, copy in wanted:
        pl.when(need)(copy.wait)
    if not start:
        for head in range(heads):
            top = packed_ref[:, base_head + head : base_head + head + 1]
            total = packed_ref[:, all_heads + base_head + head : all_heads + base_head + head + 1]
            m_ref[head] = jnp.broadcast_to(top, (rows, HEAD_DIM))
            acc_ref[head, :, HEAD_DIM:] = jnp.broadcast_to(total, (rows, HEAD_DIM))

    def scores_of(head, keys):
        if isinstance(head, int):
            at = slice(head * HEAD_DIM, (head + 1) * HEAD_DIM)
        else:
            at = pl.ds(pl.multiple_of(head * HEAD_DIM, HEAD_DIM), HEAD_DIM)
        return lax.dot_general(
            q_ref[:, at], keys, (((1,), (1,)), ((), ())), preferred_element_type=jnp.float32
        )

    def score(i, buf, mask):
        head = items[0, i]
        scores = scores_of(head, kvbuf[items[1, i], :, :HEAD_DIM])
        if mask:
            high = window[base_head + head] - items[2, i]
            seen = diff < high
            if start:
                seen = seen & (diff >= -items[2, i])
            scores = jnp.where(seen, scores, LOW)
        buf[0][...] = scores
        top = scores[:, :HEAD_DIM]
        for part in range(1, lanes):
            top = jnp.maximum(top, scores[:, part * HEAD_DIM : (part + 1) * HEAD_DIM])
        buf[1][...] = top

    def fold(head, scores, top, vaug):
        m_prev = m_ref[head]
        m_new = jnp.maximum(m_prev, jnp.max(top, axis=1, keepdims=True))
        alpha = jnp.exp2(m_prev - m_new)
        m_ref[head] = m_new
        shift = jnp.concatenate([m_new] * (scores.shape[1] // HEAD_DIM), axis=1)
        weights = jnp.exp2(scores - shift).astype(jnp.bfloat16)
        add = jnp.dot(weights, vaug, preferred_element_type=jnp.float32)
        acc_ref[head] = acc_ref[head] * jnp.concatenate([alpha, alpha], axis=1) + add

    def turns(first, last, mask):
        def turn(j, carry):
            for u in range(UNROLL):
                i = UNROLL * j + u
                score(i + 1, bufs[(u + 1) % 2], mask)
                held, top = bufs[u % 2]
                fold(items[0, i], held[...], top[...], kvbuf[items[1, i], :, HEAD_DIM:])
            return carry

        lax.fori_loop(first, last, turn, 0)

    score(0, bufs[0], True)
    turns(0, masked_turns, True)
    turns(masked_turns, all_turns, False)
    if start:
        store = pltpu.make_async_copy(acc_vmem, acc_hbm, sems.at[buffers + 1])
        store.start()
        lane = lax.broadcasted_iota(jnp.int32, (rows, HEAD_DIM), 1)
        packed = jnp.zeros((rows, HEAD_DIM), jnp.float32)
        for head in range(heads):
            packed = jnp.where(lane == head, m_ref[head], packed)
            packed = jnp.where(lane == all_heads + head, acc_ref[head, :, HEAD_DIM:], packed)
        packed_ref[...] = packed
        second = pltpu.make_async_copy(packed_ref, packed_hbm, sems.at[buffers + 2])
        second.start()
        store.wait()
        second.wait()
        return

    def give(head):
        at = pl.ds(head * HEAD_DIM, HEAD_DIM)
        return pltpu.make_async_copy(out_ref.at[:, at], out_hbm.at[:, at], sems.at[head])

    def finish(head):
        out_ref[:, head * HEAD_DIM : (head + 1) * HEAD_DIM] = (
            acc_ref[head, :, :HEAD_DIM] / acc_ref[head, :, HEAD_DIM:]
        ).astype(jnp.bfloat16)
        give(head).start()

    shortest = window[base_head]
    for head in range(1, heads):
        shortest = jnp.minimum(shortest, window[base_head + head])
    any_open = query_start + rows - 1 - shortest >= 0

    @pl.when(any_open)
    def _():
        column = lax.broadcasted_iota(jnp.int32, (rows, HEAD_DIM), 1)
        row = lax.broadcasted_iota(jnp.int32, (rows, HEAD_DIM), 0)
        pad = jnp.zeros((HEAD_DIM - SINK_ROWS, HEAD_DIM), jnp.bfloat16)
        scored, valued = [], []
        fresh = (own // QUAD) % 2 == 1
        for head in range(heads):
            base = groups[head // per_group] * PAIR
            pair = jnp.where(fresh, sink_ref[1, :, base : base + PAIR], sink_ref[0, :, base : base + PAIR])
            keys = jnp.concatenate([pair[:, :HEAD_DIM], pad], axis=0)
            values = jnp.concatenate([pair[:, HEAD_DIM:], pad], axis=0)
            valued.append(jnp.concatenate([values, jnp.ones((HEAD_DIM, HEAD_DIM), jnp.bfloat16)], axis=1))
            latest = row + (query_start - window[base_head + head])
            count = jnp.minimum(sinks[base_head + head], SINK)
            allowed = (column < count) & (column <= latest)
            scores = scores_of(head, keys) + bias[base_head + head] * LOG2E
            scored.append(jnp.where(allowed, scores, LOW))
        for head in range(heads):
            fold(head, scored[head], scored[head], valued[head])
        for head in range(heads):
            finish(head)

    @pl.when(jnp.logical_not(any_open))
    def _():
        for head in range(heads):
            finish(head)

    for head in range(heads):
        give(head).wait()


def attend(groups, all_groups, scalars, queries, arrays, sources, sinks=None, state=None):
    rows = queries.shape[0]
    key_rows = arrays[0].shape[0]
    per_group = queries.shape[1] // HEAD_DIM // all_groups
    heads = per_group * len(groups)
    buffers = len(sources) * len(groups)
    items = heads * len(sources) + 2 * UNROLL
    f32 = jnp.float32
    scratch = [
        pltpu.VMEM((rows, heads * HEAD_DIM), jnp.bfloat16),
        pltpu.VMEM((buffers, key_rows, 3 * HEAD_DIM), jnp.bfloat16),
        pltpu.SemaphoreType.DMA((buffers + 5,)),
        pltpu.SMEM((3, items), jnp.int32),
        pltpu.VMEM((rows, key_rows), f32),
        pltpu.VMEM((rows, key_rows), f32),
        pltpu.VMEM((rows, HEAD_DIM), f32),
        pltpu.VMEM((rows, HEAD_DIM), f32),
        pltpu.VMEM((heads, rows, HEAD_DIM), f32),
        pltpu.VMEM((heads, rows, PAIR), f32),
        pltpu.VMEM((rows, HEAD_DIM), f32),
    ]
    in_specs = [SMEM] * 3 + [ANY] * (1 + len(arrays))
    operands = [*scalars, queries, *arrays]
    if state is None:
        out_specs = [ANY, ANY]
        out_shape = [
            jax.ShapeDtypeStruct((heads, rows, HEAD_DIM), f32),
            jax.ShapeDtypeStruct((rows, HEAD_DIM), f32),
        ]
    else:
        in_specs += [ANY] * 4
        operands += [*sinks, *state]
        out_specs = ANY
        out_shape = jax.ShapeDtypeStruct((rows, heads * HEAD_DIM), jnp.bfloat16)
        scratch += [
            pltpu.VMEM((2, *sinks[0].shape), jnp.bfloat16),
            pltpu.VMEM((rows, heads * HEAD_DIM), jnp.bfloat16),
        ]
    return pl.pallas_call(
        functools.partial(attend_kernel, groups, per_group, sources, state is None),
        in_specs=in_specs,
        out_specs=out_specs,
        out_shape=out_shape,
        scratch_shapes=scratch,
        compiler_params=pltpu.CompilerParams(vmem_limit_bytes=ALL_VMEM),
        cost_estimate=pl.CostEstimate(
            flops=8 * rows * buffers * key_rows * per_group * HEAD_DIM,
            bytes_accessed=2 * buffers * key_rows * PAIR,
            transcendentals=rows * buffers * key_rows * per_group,
        ),
        name="attend",
    )(*operands)


def project_kernel(where, tok_ref, own0, own1, far_ref, w_ref, wa_ref, wb_ref, out_ref):
    half = own0.shape[1]
    total = jnp.dot(own0[...], w_ref[:half, :], preferred_element_type=jnp.float32)
    total += jnp.dot(own1[...], w_ref[half:, :], preferred_element_type=jnp.float32)
    total += tok_ref[...].astype(jnp.float32)
    far_dot(far_ref, wa_ref, wb_ref, out_ref, total)


def project_last_kernel(where, part_ref, far_ref, wa_ref, wb_ref, out_ref):
    far_dot(far_ref, wa_ref, wb_ref, out_ref, part_ref[...])


def far_dot(far_ref, wa_ref, wb_ref, out_ref, total):
    step, turn = pl.program_id(0), pl.num_programs(0) // 2

    @pl.when(step < turn)
    def _():
        more = jnp.dot(far_ref[...], wa_ref[...], preferred_element_type=jnp.float32)
        out_ref[...] = (total + more).astype(out_ref.dtype)

    @pl.when(step >= turn)
    def _():
        more = jnp.dot(far_ref[...], wb_ref[...], preferred_element_type=jnp.float32)
        out_ref[...] = (total + more).astype(out_ref.dtype)


def project(where, rows, share, row, own_side, far, w_near, w_swap):
    depth, _ = w_near.shape
    tile = 512
    steps = share // tile
    part = steps // 2
    half = far.shape[1]

    def column(j, where):
        return jnp.where(where[1] == 0, j, lax.rem(j + part, steps))

    here = pl.BlockSpec((rows, tile), lambda j, where: (0, column(j, where)))
    shifted = lambda height: pl.BlockSpec((height, tile), lambda j, where: (0, where[0] * steps + column(j, where)))
    fixed = lambda a: pl.BlockSpec(a.shape, lambda j, where: (0, 0))
    far_specs = [
        fixed(far),
        pl.BlockSpec((half, tile), lambda j, where: (row, jnp.minimum(j, part - 1))),
        pl.BlockSpec((half, tile), lambda j, where: (row, jnp.maximum(j - part, 0))),
    ]
    if len(own_side) > 1:
        tokens, own0, own1, w_out = own_side
        kernel, dtype = project_kernel, jnp.float32
        specs = [shifted(rows), fixed(own0), fixed(own1), far_specs[0], shifted(w_out.shape[0]), *far_specs[1:]]
        operands = [tokens, own0, own1, far, w_out, w_near, w_swap]
    else:
        kernel, dtype = project_last_kernel, jnp.bfloat16
        specs = [here, *far_specs]
        operands = [own_side[0], far, w_near, w_swap]
    return pl.pallas_call(
        kernel,
        grid_spec=pltpu.PrefetchScalarGridSpec(
            num_scalar_prefetch=1, grid=(steps,), in_specs=specs, out_specs=here
        ),
        out_shape=jax.ShapeDtypeStruct((rows, share), dtype),
        compiler_params=pltpu.CompilerParams(vmem_limit_bytes=40 * MIB),
        cost_estimate=pl.CostEstimate(
            flops=len(operands) * rows * half * share, bytes_accessed=4 * depth * share, transcendentals=0
        ),
        name="project",
    )(where, *operands)


def local(tokens, norm_gain, w_query, w_key, w_value, w_out, window, sink_count, sink_bias):
    peers = lax.axis_size("seq")
    head_peers = lax.axis_size("head")
    me = lax.axis_index("seq")
    my_head = lax.axis_index("head")
    core, side = me % 2, (me // 2) % 2
    groups = w_key.shape[1] // HEAD_DIM
    share = w_out.shape[1] // head_peers
    piece = share // 2
    gain = norm_gain.reshape(1, -1)
    everyone = range(peers)

    def send(x, pairs, axis="seq"):
        return lax.ppermute(x, axis, pairs)

    ahead = [(i, (i + QUAD) % peers) for i in everyone]
    core_swap = [(i, i ^ 1) for i in everyone]
    side_swap = [(i, i ^ 2) for i in everyone]
    head_swap = [(i, i ^ 1) for i in range(head_peers)]

    scalars = (window, sink_count, sink_bias)
    place = ((1 - my_head) * share + core * piece).astype(jnp.int32).reshape(1)

    kv, scale, w_send = keys_values(place, tokens, gain, w_key, w_value, w_out, piece)
    queries = project_queries(tokens, gain, w_query, scale)

    back4 = send(kv, ahead)
    near_side = send(kv, side_swap)
    w_near = send(w_send, head_swap, "head")
    near_core = send(kv, core_swap)
    back8 = send(back4, ahead)
    across4 = send(back4, side_swap)
    core4 = send(back4, core_swap)
    cross_near = send(near_side, core_swap)
    core8 = send(back8, core_swap)
    cross4 = send(across4, core_swap)
    far, cross_far = [], []
    for g in range(groups):
        at = slice(g * PAIR, (g + 1) * PAIR)
        part = (back8 if g % 2 == 0 else across4)[:, at]
        far.append(send(part, side_swap if g % 2 == 0 else ahead))
        cross_far.append(send(far[g], core_swap))

    top = lambda x: x[:SINK_ROWS]
    left = jnp.where(core == 0, top(kv), top(near_core))
    right = jnp.where(core == 0, top(near_side), top(cross_near))
    arrived = old = jnp.where(side == 0, left, right)
    have = peers
    while have > QUAD:
        old = arrived if have == peers else jnp.where(me % (2 * have) >= have, arrived, old)
        step = have // 2
        arrived = send(old, [(i, (i + step) % peers) for i in everyone])
        have = step
    sinks = (old, arrived)
    w_swap = send(w_near, core_swap)

    every = tuple(range(groups))
    state = attend(
        every,
        groups,
        scalars,
        queries,
        [kv, back4, core4, near_core],
        [[(a, g * PAIR) for g in every] for a in range(4)],
    )
    own, other = [], []
    for g in every:
        att = attend(
            (g,),
            groups,
            scalars,
            queries,
            [back8, across4, cross4, core8, near_side, cross_near, core4, far[g], cross_far[g]],
            [[(a, g * PAIR)] for a in range(7)] + [[(7, 0)], [(8, 0)]],
            sinks,
            state,
        )
        own.append(att)
        other.append(send(att, head_swap, "head"))
    where = jnp.stack([my_head, core]).astype(jnp.int32)
    rows = tokens.shape[0]
    partial = project(where, rows, share, 0, (tokens, *own, w_out), other[0], w_near, w_swap)
    return project(where, rows, share, 1, (partial,), other[1], w_near, w_swap)


def solution(mesh):
    in_specs = (
        P("seq", None),
        P(),
        P(None, "head"),
        P(None, "head"),
        P(None, "head"),
        P("head", None),
        P("head"),
        P("head"),
        P("head"),
    )
    out_specs = P("seq", "head")
    return jax.shard_map(local, mesh=mesh, in_specs=in_specs, out_specs=out_specs, check_vma=False)
```

```python
import functools

import jax
import jax.numpy as jnp
from jax import lax
from jax.experimental import pallas as pl
from jax.experimental.pallas import tpu as pltpu
from jax.sharding import PartitionSpec as P


HEAD_DIM = 128
PAIR = 2 * HEAD_DIM
SINK = 4
SINK_ROWS = 16
SPAN = 9
QUAD = (SPAN - 1) // 2
EPSILON = 1e-05
LOG2E = 1.4426950408889634
LOW = -1e30
UNROLL = 2
NOWHERE = 1 << 20
MIB = 1024 * 1024
ALL_VMEM = 67043328 - 128 * 1024
ANY = pl.BlockSpec(memory_space=pltpu.HBM)
SMEM = pl.BlockSpec(memory_space=pltpu.SMEM)
VMEM = pl.BlockSpec(memory_space=pltpu.VMEM)


def keys_values_kernel(place, tok_ref, gain_ref, wk_ref, wv_ref, w_hbm, *refs):
    groups = wk_ref.shape[1] // HEAD_DIM
    kv_ref, scale_ref, send_hbm, k_acc, v_acc, squares, w_vmem, sem_in, sem_out = refs
    step, steps = pl.program_id(0), pl.num_programs(0)
    piece = send_hbm.shape[1]
    columns = pl.ds(pl.multiple_of(place[0], HEAD_DIM), piece)
    fetch = pltpu.make_async_copy(w_hbm.at[:, columns], w_vmem, sem_in)
    store = pltpu.make_async_copy(w_vmem, send_hbm, sem_out)

    @pl.when(step == 0)
    def _():
        fetch.start()
        k_acc[...] = jnp.zeros(k_acc.shape, jnp.float32)
        v_acc[...] = jnp.zeros(v_acc.shape, jnp.float32)
        squares[...] = jnp.zeros(squares.shape, jnp.float32)

    @pl.when(step == steps // 2)
    def _():
        fetch.wait()
        store.start()

    widened = tok_ref[...].astype(jnp.float32)
    scaled = (widened * gain_ref[...]).astype(jnp.bfloat16)
    k_acc[...] += jnp.dot(scaled, wk_ref[...], preferred_element_type=jnp.float32)
    v_acc[...] += jnp.dot(scaled, wv_ref[...], preferred_element_type=jnp.float32)
    square = widened * widened
    total = square[:, :HEAD_DIM]
    for lo in range(HEAD_DIM, square.shape[1], HEAD_DIM):
        total += square[:, lo : lo + HEAD_DIM]
    squares[...] += total

    @pl.when(step == steps - 1)
    def _():
        mean = jnp.sum(squares[...], axis=1, keepdims=True) / (steps * tok_ref.shape[1])
        scale = jnp.broadcast_to(lax.rsqrt(mean + EPSILON), scale_ref.shape)
        scale_ref[...] = scale
        for g in range(groups):
            at = slice(g * HEAD_DIM, (g + 1) * HEAD_DIM)
            pair = jnp.concatenate([k_acc[:, at] * scale, v_acc[:, at] * scale], axis=1).astype(jnp.bfloat16)
            kv_ref[:, g * PAIR : (g + 1) * PAIR] = pair
        store.wait()


def keys_values(place, tokens, gain, w_key, w_value, w_out, piece):
    rows, width = tokens.shape
    narrow = w_key.shape[1]
    groups = narrow // HEAD_DIM
    chunk = width // 4
    fixed = lambda shape: pl.BlockSpec(shape, lambda i, place: (0, 0))
    return pl.pallas_call(
        keys_values_kernel,
        grid_spec=pltpu.PrefetchScalarGridSpec(
            num_scalar_prefetch=1,
            grid=(width // chunk,),
            in_specs=[
                pl.BlockSpec((rows, chunk), lambda i, place: (0, i)),
                pl.BlockSpec((1, chunk), lambda i, place: (0, i)),
                pl.BlockSpec((chunk, narrow), lambda i, place: (i, 0)),
                pl.BlockSpec((chunk, narrow), lambda i, place: (i, 0)),
                ANY,
            ],
            out_specs=[fixed((rows, groups * PAIR))]
            + [fixed((rows, HEAD_DIM)), ANY],
            scratch_shapes=[
                pltpu.VMEM((rows, narrow), jnp.float32),
                pltpu.VMEM((rows, narrow), jnp.float32),
                pltpu.VMEM((rows, HEAD_DIM), jnp.float32),
                pltpu.VMEM((w_out.shape[0], piece), jnp.bfloat16),
                pltpu.SemaphoreType.DMA,
                pltpu.SemaphoreType.DMA,
            ],
        ),
        out_shape=[jax.ShapeDtypeStruct((rows, groups * PAIR), jnp.bfloat16)]
        + [
            jax.ShapeDtypeStruct((rows, HEAD_DIM), jnp.float32),
            jax.ShapeDtypeStruct((w_out.shape[0], piece), jnp.bfloat16),
        ],
        compiler_params=pltpu.CompilerParams(vmem_limit_bytes=60 * MIB),
        cost_estimate=pl.CostEstimate(
            flops=4 * rows * width * narrow, bytes_accessed=2 * width * (rows + 2 * narrow), transcendentals=rows
        ),
        name="keys_values",
    )(place, tokens, gain, w_key, w_value, w_out)


def query_kernel(tok_ref, gain_ref, w_ref, scale_ref, q_ref, acc):
    step = pl.program_id(0)
    scaled = (tok_ref[...].astype(jnp.float32) * gain_ref[...]).astype(jnp.bfloat16)
    add = jnp.dot(scaled, w_ref[...], preferred_element_type=jnp.float32)

    @pl.when(step == 0)
    def _():
        acc[...] = add

    @pl.when(step > 0)
    def _():
        acc[...] += add

    @pl.when(step == pl.num_programs(0) - 1)
    def _():
        scale = scale_ref[...] * (HEAD_DIM**-0.5 * LOG2E)
        scale = jnp.concatenate([scale] * (acc.shape[1] // HEAD_DIM), axis=1)
        q_ref[...] = (acc[...] * scale).astype(jnp.bfloat16)


def project_queries(tokens, gain, w_query, scale):
    rows, width = tokens.shape
    share = w_query.shape[1]
    chunk = width // 4
    return pl.pallas_call(
        query_kernel,
        grid=(width // chunk,),
        in_specs=[
            pl.BlockSpec((rows, chunk), lambda i: (0, i)),
            pl.BlockSpec((1, chunk), lambda i: (0, i)),
            pl.BlockSpec((chunk, share), lambda i: (i, 0)),
            pl.BlockSpec(scale.shape, lambda i: (0, 0)),
        ],
        out_specs=pl.BlockSpec((rows, share), lambda i: (0, 0)),
        out_shape=jax.ShapeDtypeStruct((rows, share), jnp.bfloat16),
        scratch_shapes=[pltpu.VMEM((rows, share), jnp.float32)],
        compiler_params=pltpu.CompilerParams(vmem_limit_bytes=58 * MIB),
        cost_estimate=pl.CostEstimate(
            flops=2 * rows * width * share, bytes_accessed=2 * width * (rows + share), transcendentals=0
        ),
        name="queries",
    )(tokens, gain, w_query, scale)


def stay(*arrays):
    return [pltpu.with_memory_space_constraint(a, pltpu.HBM) for a in arrays]


def early_blocks(me):
    twin, core = me ^ 1, me % 2
    return [me, me - 4, jnp.where(core == 0, twin - 4, -1), jnp.where(core == 1, twin, -1)]


def late_blocks(me):
    twin, across, mirror = me ^ 1, me ^ 2, me ^ 3
    core, side = me % 2, (me // 2) % 2
    return [
        me - 8,
        across - 4,
        mirror - 4,
        jnp.where(core == 0, twin - 8, -1),
        jnp.where(side == 1, across, -1),
        jnp.where(side == 1, mirror, -1),
        jnp.where(core == 1, twin - 4, -1),
        jnp.where(side == 0, across - 8, -1),
        jnp.where(side == 0, mirror - 8, -1),
    ]


def attend_kernel(groups, per_group, base_head, sources, start, extra, *refs):
    window, sinks, bias, q_hbm = refs[:4]
    sent = 1 + max(ref for slot in sources for ref, _ in slot)
    kv_refs, refs = refs[4 : 4 + sent], refs[4 + sent :]
    if start:
        acc_hbm, packed_hbm = refs[:2]
        refs = refs[2:]
    else:
        sink_old, sink_new, acc_hbm, packed_hbm = refs[:4]
        sources_ahead, out_hbm = refs[4 : 4 + extra], refs[4 + extra]
        targets_ahead, refs = refs[5 + extra : 5 + 2 * extra], refs[5 + 2 * extra :]
        sink_ref, out_ref = refs[-2:]
        refs = refs[:-2]
    q_ref, kvbuf, sems, items, s_even, s_odd, x_even, x_odd, m_ref, acc_ref, packed_ref = refs
    bufs = ((s_even, x_even), (s_odd, x_odd))
    rows, key_rows = q_ref.shape[0], kvbuf.shape[1]
    share, buffers = len(groups), kvbuf.shape[0]
    heads = share * per_group
    all_heads = acc_hbm.shape[0]
    lanes = key_rows // HEAD_DIM
    own = lax.axis_index("seq")
    query_start = own * rows
    table = early_blocks(own) if start else late_blocks(own)
    acc_vmem = acc_ref.at[:, :, pl.ds(0, HEAD_DIM)]
    copies = [
        pltpu.make_async_copy(
            q_hbm.at[:, pl.ds(base_head * HEAD_DIM, heads * HEAD_DIM)], q_ref, sems.at[buffers]
        )
    ]
    if not start:
        copies += [
            pltpu.make_async_copy(acc_hbm.at[pl.ds(base_head, heads)], acc_vmem, sems.at[buffers + 1]),
            pltpu.make_async_copy(packed_hbm, packed_ref, sems.at[buffers + 2]),
            pltpu.make_async_copy(sink_old, sink_ref.at[0], sems.at[buffers + 3]),
            pltpu.make_async_copy(sink_new, sink_ref.at[1], sems.at[buffers + 4]),
        ]
    longest = [window[base_head + g * per_group] for g in range(share)]
    for g in range(share):
        for head in range(1, per_group):
            longest[g] = jnp.maximum(longest[g], window[base_head + g * per_group + head])
    wanted = []
    for s, slot in enumerate(sources):
        for g, (ref, column) in enumerate(slot):
            need = (table[s] >= 0) & ((own - table[s]) * rows - (rows - 1) < longest[g])
            copy = pltpu.make_async_copy(
                kv_refs[ref].at[:, pl.ds(column, PAIR)],
                kvbuf.at[s * share + g, :, pl.ds(0, PAIR)],
                sems.at[s * share + g],
            )
            wanted.append((need, copy))
            pl.when(need)(copy.start)
    for copy in copies:
        copy.start()
    ahead = []
    if not start and extra:
        for i, (source, target) in enumerate(zip(sources_ahead, targets_ahead)):
            width = target.shape[1]
            columns = pl.ds(pl.multiple_of(lax.axis_index("head") * width, width), width)
            ahead.append(pltpu.make_async_copy(source.at[:, columns], target, sems.at[buffers + 5 + i]))
            ahead[-1].start()
    kvbuf[:, :, PAIR:] = jnp.ones((buffers, key_rows, HEAD_DIM), jnp.bfloat16)
    if start:
        m_ref[...] = jnp.full(m_ref.shape, LOW, jnp.float32)
        acc_ref[...] = jnp.zeros(acc_ref.shape, jnp.float32)

    def put(n, head, kv, gap):
        items[0, n] = head
        items[1, n] = kv
        items[2, n] = gap

    def scan(s, block, n, want_whole):
        gap = (own - block) * rows

        def add(head, n):
            reach = window[base_head + head]
            put(n, head, s * share + head // per_group, gap)
            some = gap - (rows - 1) < reach
            whole = (gap > 0) & (gap + rows - 1 < reach)
            return n + (whole if want_whole else some & jnp.logical_not(whole)).astype(jnp.int32)

        return lax.fori_loop(0, jnp.where(block >= 0, heads, 0), add, n)

    n = jnp.int32(0)
    for s, block in enumerate(table):
        n = scan(s, block, n, False)
    masked = n
    for s, block in enumerate(table):
        n = scan(s, block, n, True)
    odd = lax.rem(n, UNROLL)

    @pl.when(odd > 0)
    def _():
        loaded = items[1, 0]

        def shift(k, carry):
            for row in range(3):
                items[row, n - k] = items[row, n - k - 1]
            return carry

        lax.fori_loop(0, n - masked, shift, 0)
        put(masked, 0, loaded, NOWHERE)

    masked_turns = (masked + odd + UNROLL - 1) // UNROLL
    all_turns = (n + odd) // UNROLL
    put(n + odd, 0, 0, NOWHERE)
    diff = lax.broadcasted_iota(jnp.int32, (rows, key_rows), 0) - lax.broadcasted_iota(
        jnp.int32, (rows, key_rows), 1
    )
    for copy in copies:
        copy.wait()
    for need, copy in wanted:
        pl.when(need)(copy.wait)
    if not start:
        for head in range(heads):
            top = packed_ref[:, base_head + head : base_head + head + 1]
            total = packed_ref[:, all_heads + base_head + head : all_heads + base_head + head + 1]
            m_ref[head] = jnp.broadcast_to(top, (rows, HEAD_DIM))
            acc_ref[head, :, HEAD_DIM:] = jnp.broadcast_to(total, (rows, HEAD_DIM))

    def scores_of(head, keys):
        if isinstance(head, int):
            at = slice(head * HEAD_DIM, (head + 1) * HEAD_DIM)
        else:
            at = pl.ds(pl.multiple_of(head * HEAD_DIM, HEAD_DIM), HEAD_DIM)
        return lax.dot_general(
            q_ref[:, at], keys, (((1,), (1,)), ((), ())), preferred_element_type=jnp.float32
        )

    def score(i, buf, mask):
        head = items[0, i]
        scores = scores_of(head, kvbuf[items[1, i], :, :HEAD_DIM])
        if mask:
            high = window[base_head + head] - items[2, i]
            seen = diff < high
            if start:
                seen = seen & (diff >= -items[2, i])
            scores = jnp.where(seen, scores, LOW)
        buf[0][...] = scores
        top = scores[:, :HEAD_DIM]
        for part in range(1, lanes):
            top = jnp.maximum(top, scores[:, part * HEAD_DIM : (part + 1) * HEAD_DIM])
        buf[1][...] = top

    def fold(head, scores, top, vaug):
        m_prev = m_ref[head]
        m_new = jnp.maximum(m_prev, jnp.max(top, axis=1, keepdims=True))
        alpha = jnp.exp2(m_prev - m_new)
        m_ref[head] = m_new
        shift = jnp.concatenate([m_new] * (scores.shape[1] // HEAD_DIM), axis=1)
        weights = jnp.exp2(scores - shift).astype(jnp.bfloat16)
        add = jnp.dot(weights, vaug, preferred_element_type=jnp.float32)
        acc_ref[head] = acc_ref[head] * jnp.concatenate([alpha, alpha], axis=1) + add

    def turns(first, last, mask):
        def turn(j, carry):
            for u in range(UNROLL):
                i = UNROLL * j + u
                score(i + 1, bufs[(u + 1) % 2], mask)
                held, top = bufs[u % 2]
                fold(items[0, i], held[...], top[...], kvbuf[items[1, i], :, HEAD_DIM:])
            return carry

        lax.fori_loop(first, last, turn, 0)

    score(0, bufs[0], True)
    turns(0, masked_turns, True)
    turns(masked_turns, all_turns, False)
    if start:
        store = pltpu.make_async_copy(acc_vmem, acc_hbm, sems.at[buffers + 1])
        store.start()
        lane = lax.broadcasted_iota(jnp.int32, (rows, HEAD_DIM), 1)
        packed = jnp.zeros((rows, HEAD_DIM), jnp.float32)
        for head in range(heads):
            packed = jnp.where(lane == head, m_ref[head], packed)
            packed = jnp.where(lane == all_heads + head, acc_ref[head, :, HEAD_DIM:], packed)
        packed_ref[...] = packed
        second = pltpu.make_async_copy(packed_ref, packed_hbm, sems.at[buffers + 2])
        second.start()
        store.wait()
        second.wait()
        return

    def give(head):
        at = pl.ds(head * HEAD_DIM, HEAD_DIM)
        return pltpu.make_async_copy(out_ref.at[:, at], out_hbm.at[:, at], sems.at[head])

    def finish(head):
        out_ref[:, head * HEAD_DIM : (head + 1) * HEAD_DIM] = (
            acc_ref[head, :, :HEAD_DIM] / acc_ref[head, :, HEAD_DIM:]
        ).astype(jnp.bfloat16)
        give(head).start()

    shortest = window[base_head]
    for head in range(1, heads):
        shortest = jnp.minimum(shortest, window[base_head + head])
    any_open = query_start + rows - 1 - shortest >= 0

    @pl.when(any_open)
    def _():
        column = lax.broadcasted_iota(jnp.int32, (rows, HEAD_DIM), 1)
        row = lax.broadcasted_iota(jnp.int32, (rows, HEAD_DIM), 0)
        pad = jnp.zeros((HEAD_DIM - SINK_ROWS, HEAD_DIM), jnp.bfloat16)
        scored, valued = [], []
        fresh = (own // QUAD) % 2 == 1
        for head in range(heads):
            base = groups[head // per_group] * PAIR
            pair = jnp.where(fresh, sink_ref[1, :, base : base + PAIR], sink_ref[0, :, base : base + PAIR])
            keys = jnp.concatenate([pair[:, :HEAD_DIM], pad], axis=0)
            values = jnp.concatenate([pair[:, HEAD_DIM:], pad], axis=0)
            valued.append(jnp.concatenate([values, jnp.ones((HEAD_DIM, HEAD_DIM), jnp.bfloat16)], axis=1))
            latest = row + (query_start - window[base_head + head])
            count = jnp.minimum(sinks[base_head + head], SINK)
            allowed = (column < count) & (column <= latest)
            scores = scores_of(head, keys) + bias[base_head + head] * LOG2E
            scored.append(jnp.where(allowed, scores, LOW))
        for head in range(heads):
            fold(head, scored[head], scored[head], valued[head])
        for head in range(heads):
            finish(head)

    @pl.when(jnp.logical_not(any_open))
    def _():
        for head in range(heads):
            finish(head)

    for head in range(heads):
        give(head).wait()
    for copy in ahead:
        copy.wait()


def attend(groups, per_group, base_head, scalars, queries, arrays, sources, sinks=None, state=None, ahead=(), share=0):
    rows = queries.shape[0]
    key_rows = arrays[0].shape[0]
    heads = per_group * len(groups)
    buffers = len(sources) * len(groups)
    items = heads * len(sources) + 2 * UNROLL
    f32 = jnp.float32
    scratch = [
        pltpu.VMEM((rows, heads * HEAD_DIM), jnp.bfloat16),
        pltpu.VMEM((buffers, key_rows, 3 * HEAD_DIM), jnp.bfloat16),
        pltpu.SemaphoreType.DMA((buffers + 5 + len(ahead),)),
        pltpu.SMEM((3, items), jnp.int32),
        pltpu.VMEM((rows, key_rows), f32),
        pltpu.VMEM((rows, key_rows), f32),
        pltpu.VMEM((rows, HEAD_DIM), f32),
        pltpu.VMEM((rows, HEAD_DIM), f32),
        pltpu.VMEM((heads, rows, HEAD_DIM), f32),
        pltpu.VMEM((heads, rows, PAIR), f32),
        pltpu.VMEM((rows, HEAD_DIM), f32),
    ]
    in_specs = [SMEM] * 3 + [ANY] * (1 + len(arrays))
    operands = [*scalars, *stay(queries, *arrays)]
    if state is None:
        out_specs = [ANY, ANY]
        out_shape = [
            jax.ShapeDtypeStruct((heads, rows, HEAD_DIM), f32),
            jax.ShapeDtypeStruct((rows, HEAD_DIM), f32),
        ]
    else:
        in_specs += [ANY] * (4 + len(ahead))
        operands += stay(*sinks, *state, *ahead)
        out_specs = [ANY] + [VMEM] * len(ahead)
        out_shape = [jax.ShapeDtypeStruct((rows, heads * HEAD_DIM), jnp.bfloat16)]
        out_shape += [jax.ShapeDtypeStruct((a.shape[0], share), a.dtype) for a in ahead]
        scratch += [
            pltpu.VMEM((2, *sinks[0].shape), jnp.bfloat16),
            pltpu.VMEM((rows, heads * HEAD_DIM), jnp.bfloat16),
        ]
    return pl.pallas_call(
        functools.partial(attend_kernel, groups, per_group, base_head, sources, state is None, len(ahead)),
        in_specs=in_specs,
        out_specs=out_specs,
        out_shape=out_shape,
        scratch_shapes=scratch,
        compiler_params=pltpu.CompilerParams(vmem_limit_bytes=40 * MIB if ahead else ALL_VMEM),
        cost_estimate=pl.CostEstimate(
            flops=8 * rows * buffers * key_rows * per_group * HEAD_DIM,
            bytes_accessed=2 * buffers * key_rows * PAIR,
            transcendentals=rows * buffers * key_rows * per_group,
        ),
        name="attend",
    )(*operands)


TILE = 512


def wide_copies(w_near, w_swap, row, w_buf, sems):
    piece, depth = w_near.shape[1], w_buf.shape[0]
    core = lax.axis_index("seq") % 2
    places = [pl.multiple_of(core * piece, piece), pl.multiple_of((1 - core) * piece, piece)]
    return [
        pltpu.make_async_copy(
            w.at[pl.ds(row, depth), :], w_buf.at[:, pl.ds(place, piece)], sems.at[i]
        )
        for i, (w, place) in enumerate(zip((w_near, w_swap), places))
    ]


def project_kernel(counts, tok, w_own, *refs):
    own, refs = refs[: counts[0]], refs[counts[0] :]
    far, refs = refs[: counts[1]], refs[counts[1] :]
    w_near, w_swap, part, w_last, lhs, far_buf, w_far, sems, near_sems, last_sems = refs
    tiles = part.shape[1] // TILE
    loads, at = [], 0
    for i, ref in enumerate(own):
        loads.append(pltpu.make_async_copy(ref, lhs.at[:, pl.ds(at, ref.shape[1])], sems.at[i]))
        at += ref.shape[1]
    late, at = [], 0
    for i, ref in enumerate(far):
        late.append(
            pltpu.make_async_copy(ref, far_buf.at[:, pl.ds(at, ref.shape[1])], sems.at[len(own) + i])
        )
        at += ref.shape[1]
    late += wide_copies(w_near, w_swap, 0, w_far, near_sems)
    last = wide_copies(w_near, w_swap, at, w_last, last_sems)
    for copy in loads + late + last:
        copy.start()
    for copy in loads:
        copy.wait()
    for t in range(tiles):
        here = slice(t * TILE, (t + 1) * TILE)
        total = jnp.dot(lhs[...], w_own[:, here], preferred_element_type=jnp.float32)
        part[:, here] = tok[:, here].astype(jnp.float32) + total
    for copy in late:
        copy.wait()
    for t in range(tiles):
        here = slice(t * TILE, (t + 1) * TILE)
        part[:, here] += jnp.dot(far_buf[...], w_far[:, here], preferred_element_type=jnp.float32)
    for copy in last:
        copy.wait()


def project_last_kernel(part, far, w_last, out, out_buf, sems):
    stores = []
    for t in range(out.shape[1] // TILE):
        here = slice(t * TILE, (t + 1) * TILE)
        more = jnp.dot(far[...], w_last[:, here], preferred_element_type=jnp.float32)
        out_buf[:, here] = (part[:, here] + more).astype(jnp.bfloat16)
        at = pl.ds(t * TILE, TILE)
        stores.append(pltpu.make_async_copy(out_buf.at[:, at], out.at[:, at], sems.at[t]))
        stores[-1].start()
    for store in stores:
        store.wait()


def project(tokens, w_own, own, far, w_near, w_swap):
    rows, share = tokens.shape
    depth = w_own.shape[0]
    known = sum(x.shape[1] for x in far)
    bf16 = jnp.bfloat16
    return pl.pallas_call(
        functools.partial(project_kernel, (len(own), len(far))),
        in_specs=[VMEM] * 2 + [ANY] * (2 + len(own) + len(far)),
        out_specs=[VMEM, VMEM],
        out_shape=[
            jax.ShapeDtypeStruct((rows, share), jnp.float32),
            jax.ShapeDtypeStruct((w_near.shape[0] - known, share), bf16),
        ],
        scratch_shapes=[
            pltpu.VMEM((rows, depth), bf16),
            pltpu.VMEM((rows, known), bf16),
            pltpu.VMEM((known, share), bf16),
            pltpu.SemaphoreType.DMA((len(own) + len(far),)),
            pltpu.SemaphoreType.DMA((2,)),
            pltpu.SemaphoreType.DMA((2,)),
        ],
        compiler_params=pltpu.CompilerParams(vmem_limit_bytes=40 * MIB),
        cost_estimate=pl.CostEstimate(
            flops=2 * rows * (depth + known) * share, bytes_accessed=2 * known * share, transcendentals=0
        ),
        name="project",
    )(tokens, w_own, *stay(*own, *far, w_near, w_swap))


def project_last(partial, far, w_last):
    rows, share = partial.shape
    return pl.pallas_call(
        project_last_kernel,
        in_specs=[VMEM] * 3,
        out_specs=ANY,
        out_shape=jax.ShapeDtypeStruct((rows, share), jnp.bfloat16),
        scratch_shapes=[
            pltpu.VMEM((rows, share), jnp.bfloat16),
            pltpu.SemaphoreType.DMA((share // TILE,)),
        ],
        compiler_params=pltpu.CompilerParams(vmem_limit_bytes=24 * MIB),
        cost_estimate=pl.CostEstimate(
            flops=2 * rows * far.shape[1] * share, bytes_accessed=2 * rows * share, transcendentals=0
        ),
        name="project_last",
    )(partial, far, w_last)


def local(tokens, norm_gain, w_query, w_key, w_value, w_out, window, sink_count, sink_bias):
    peers = lax.axis_size("seq")
    head_peers = lax.axis_size("head")
    me = lax.axis_index("seq")
    my_head = lax.axis_index("head")
    core, side = me % 2, (me // 2) % 2
    groups = w_key.shape[1] // HEAD_DIM
    share = w_out.shape[1] // head_peers
    piece = share // 2
    gain = norm_gain.reshape(1, -1)
    everyone = range(peers)

    def send(x, pairs, axis="seq"):
        return lax.ppermute(x, axis, pairs)

    ahead = [(i, (i + QUAD) % peers) for i in everyone]
    core_swap = [(i, i ^ 1) for i in everyone]
    side_swap = [(i, i ^ 2) for i in everyone]
    head_swap = [(i, i ^ 1) for i in range(head_peers)]

    scalars = (window, sink_count, sink_bias)
    place = ((1 - my_head) * share + core * piece).astype(jnp.int32).reshape(1)

    kv, scale, w_send = keys_values(place, tokens, gain, w_key, w_value, w_out, piece)
    queries = project_queries(tokens, gain, w_query, scale)

    back4 = send(kv, ahead)
    near_side = send(kv, side_swap)
    w_near = send(w_send, head_swap, "head")
    near_core = send(kv, core_swap)
    back8 = send(back4, ahead)
    across4 = send(back4, side_swap)
    core4 = send(back4, core_swap)
    cross_near = send(near_side, core_swap)
    core8 = send(back8, core_swap)
    cross4 = send(across4, core_swap)
    far, cross_far = [], []
    for g in range(groups):
        at = slice(g * PAIR, (g + 1) * PAIR)
        part = (back8 if g % 2 == 0 else across4)[:, at]
        far.append(send(part, side_swap if g % 2 == 0 else ahead))
        cross_far.append(send(far[g], core_swap))

    top = lambda x: x[:SINK_ROWS]
    left = jnp.where(core == 0, top(kv), top(near_core))
    right = jnp.where(core == 0, top(near_side), top(cross_near))
    arrived = old = jnp.where(side == 0, left, right)
    have = peers
    while have > QUAD:
        old = arrived if have == peers else jnp.where(me % (2 * have) >= have, arrived, old)
        step = have // 2
        arrived = send(old, [(i, (i + step) % peers) for i in everyone])
        have = step
    sinks = (old, arrived)
    w_swap = send(w_near, core_swap)

    every = tuple(range(groups))
    per_group = queries.shape[1] // HEAD_DIM // groups
    state = attend(
        every,
        per_group,
        0,
        scalars,
        queries,
        [kv, back4, core4, near_core],
        [[(a, g * PAIR) for g in every] for a in range(4)],
    )
    chunks = [(g, g * per_group, per_group) for g in every[:-1]]
    g, half = every[-1], per_group // 2
    chunks += [(g, g * per_group, half), (g, g * per_group + half, half)]
    own, other = [], []
    for c, (g, base_head, count) in enumerate(chunks):
        att = attend(
            (g,),
            count,
            base_head,
            scalars,
            queries,
            [back8, across4, cross4, core8, near_side, cross_near, core4, far[g], cross_far[g]],
            [[(a, g * PAIR)] for a in range(7)] + [[(7, 0)], [(8, 0)]],
            sinks,
            state,
            (tokens, w_out) if c == len(chunks) - 1 else (),
            share,
        )
        att, early = att[0], att[1:]
        own.append(att)
        other.append(send(att, head_swap, "head"))
    partial, w_last = project(*early, own, other[:-1], w_near, w_swap)
    return project_last(partial, other[-1], w_last)


def solution(mesh):
    in_specs = (
        P("seq", None),
        P(),
        P(None, "head"),
        P(None, "head"),
        P(None, "head"),
        P("head", None),
        P("head"),
        P("head"),
        P("head"),
    )
    out_specs = P("seq", "head")
    return jax.shard_map(local, mesh=mesh, in_specs=in_specs, out_specs=out_specs, check_vma=False)
```
